32 devices in a mesh: groups: 2 (over y), expert: 4 (over z), tensor: 2 (over x), dp: 2 (over core).
Axes of the slice: x: 2, y: 2, z: 4, core: 2. Of those that a mesh axis runs over, the one named last changes fastest.
Arguments:
- attn: bfloat16 [1024, 4096], P(('groups', 'expert', 'dp'), 'tensor'), parts along dimension 0, may hold values from -6 to 6
- o_weight: bfloat16 [4096, 4096], P('tensor', 'dp'), may hold values from -0.09375 to 0.09375
- residual: bfloat16 [1024, 4096], P(('groups', 'expert', 'dp'), 'tensor'), parts along dimension 0, may hold values from -100 to 100
- norm_gain: bfloat16 [4096], replicated, may hold values from 0.099609375 to 1.8984375
- expert_ids: int32 [1024, 8], P(('groups', 'expert', 'dp')), parts along dimension 0, may hold values from 0 to 31, all different within a row; in each aligned block of 64 rows (0 to 63, 64 to 127, ...) at most 24 rows name the same one
- route_weights: float32 [1024, 8], P(('groups', 'expert', 'dp')), parts along dimension 0, may hold values from 0.1 to 1
- w_gate: bfloat16 [32, 4096, 1024], P(('expert', 'dp'), None, 'tensor'), may hold values from -0.09375 to 0.09375
- w_up: bfloat16 [32, 4096, 1024], P(('expert', 'dp'), None, 'tensor'), may hold values from -0.09375 to 0.09375
- w_down: bfloat16 [32, 1024, 4096], P(('expert', 'dp'), 'tensor'), may hold values from -0.25 to 0.25
Outputs:
- moe_out: bfloat16 [1024, 4096], P(('groups', 'expert', 'dp'), 'tensor'), parts along dimension 0
The draws below stay inside these ranges and needn't reach their ends.
There are 2 independent parts, one for each index of `groups`. The reference program is written for one: setup_inputs(seed, part) draws one part's arguments, and reference() takes and returns one part's arrays. A program takes and returns all parts, laid end to end along the dimension named above; an argument that names none is the same for every part. Nothing has to cross between parts.
Inputs may be any that keep to these rules, and one draw needn't show every extreme that they name: `expert_ids`: each row names 8 different experts. Within each aligned block of 64 rows (the rows of one device) no expert is named by more than 24 rows, and in every draw some block has an expert named by exactly 24 rows.
All inputs are finite; a program needn't handle non-finite values.
Results may differ from the reference program's by a relative error of at most 0.024.
Values may be sent and summed in bfloat16 or wider, within the bound.
No kernel may reach another device: no remote copies, remote signals or barrier semaphores. Data moves between devices by JAX's collectives and lax.ppermute only.
A program may use at most 128 MiB of HBM per device.

```python
import math
import jax
import jax.numpy as jnp
import numpy as np
from jax import lax

D = 4096
HA = 4096
FF = 1024
EXPERTS = 32
TOPK = 8
ROWS_DEV = 64
SLOT = 24
ROWS = 512
FF_PART = 512
N_TENSOR = 2


def draw_residual(key, part):
    key_base, key_row = jax.random.split(jax.random.fold_in(key, 17), 2)
    column_scale = 0.3 * 10.0 ** (jnp.arange(D, dtype=jnp.float32) / D)
    base = jax.random.normal(key_base, (ROWS, D), jnp.float32)
    row_scale = jnp.exp(jax.random.uniform(key_row, (ROWS, 1), jnp.float32, jnp.log(0.5), jnp.log(5.0)))
    return jnp.clip(base * row_scale * column_scale[None, :], -100.0, 100.0).astype(jnp.bfloat16)


def with_spikes(entries, key, source, target, blocks, factor):
    owner, partner = [(jnp.arange(entries.shape[position]) // (entries.shape[position] // blocks)).reshape([-1 if axis == position else 1 for axis in range(entries.ndim)]) for position in (source, target)]
    chosen = jax.random.permutation(key, blocks)[partner]
    strong = (owner == chosen) | (owner == (partner + blocks // 2) % blocks)
    return jnp.where(strong, factor * entries, entries)


def level_of(stream_key, shape, pieces, smallest, high):
    level = 1.0
    for dim, parts in pieces:
        draws = jax.random.uniform(jax.random.fold_in(jax.random.fold_in(stream_key, 6), dim), (parts,), jnp.float32, smallest / len(pieces), high / len(pieces))
        level = level * jnp.repeat(jnp.exp(draws), shape[dim] // parts).reshape((-1,) + (1,) * (len(shape) - 1 - dim))
    return level


def deal_out(key, own, number, rows, number_of, top, most, lean):
    sequence = jax.random.permutation(key, number_of)
    crowded, ordinary = portions_of(number_of, rows * top, most, lean, True), portions_of(number_of, rows * top, most, lean, False)
    places = jnp.arange(number_of)

    def named(lengths, turn):
        used = int((lengths > 0).sum())
        fixed = max(1, used // 4)
        passed = fixed + (places - fixed + turn * (used - fixed)) % max(1, number_of - fixed)
        return jnp.zeros((number_of,), jnp.int32).at[sequence[jnp.where(places < fixed, places, passed)]].set(jnp.asarray(lengths, jnp.int32))

    lengths = jnp.where(number % 4 == 0, named(crowded, number // 4), named(ordinary, number - number // 4 - 1))
    mixed = jax.random.permutation(jax.random.fold_in(own, 3), number_of)
    giver, sink = mixed[0:number_of // 2 * 2:2], mixed[1:number_of // 2 * 2:2]
    margin = jnp.minimum(lengths[giver] - 1, most - lengths[sink]) // 2
    margin = jnp.where((giver == sequence[0]) | (sink == sequence[0]) | (lengths[sink] == 0), 0, jnp.maximum(margin, 0))
    passed = jax.random.randint(jax.random.fold_in(own, 4), (number_of // 2,), 0, 1 << 20) % (margin + 1)
    lengths = lengths.at[giver].add(-passed).at[sink].add(passed)
    items = jnp.searchsorted(jnp.cumsum(lengths), jnp.arange(rows * top), side="right").astype(jnp.int32)
    table = items.reshape(top, rows).T
    table = table[jax.random.permutation(jax.random.fold_in(own, 1), rows)]
    turn = jax.random.randint(jax.random.fold_in(own, 2), (rows, 1), 0, top)
    return jnp.take_along_axis(table, (jnp.arange(top)[None, :] + turn) % top, axis=1)


def portions_of(count, total, limit, lean, full):
    portions = [(1 << 20) // math.isqrt(standing ** lean) + 1 for standing in range(1, count + 1)]
    largest = limit if full else min(limit, max(-(-total // count), total * portions[0] // sum(portions)))
    least = 1 if total - largest >= count - 1 else 0
    given, rest = [largest] + [least] * (count - 1), total - largest - least * (count - 1)
    while rest > 0:
        movable = [i for i in range(1, count) if given[i] < largest] or [i for i in range(1, count) if given[i] < limit]
        mass, budget = sum([portions[i] for i in movable]), rest
        for i in movable:
            addition = min(limit - given[i], max(1, budget * portions[i] // mass), rest)
            given[i] = given[i] + addition
            rest = rest - addition
    return np.array(given)


def gaussian(stream_key, shape, spread, most, pieces=(), held_as=jnp.bfloat16):
    entries = jax.random.normal(stream_key, shape, jnp.float32) * spread
    if len(pieces) > 0:
        entries = level_of(stream_key, shape, pieces, -0.22, 0.18) * entries
    return jnp.clip(entries, min=-most, max=most).astype(held_as)


def bell_draw_with(rng, extent, width, limit, shards, heavy, held_as=jnp.bfloat16):
    array = width * jax.random.normal(rng, extent, jnp.float32)
    if shards:
        array = array * level_of(rng, extent, shards, -0.22, 0.18)
    return jnp.clip(with_spikes(array, jax.random.fold_in(rng, 3), *heavy), -limit, limit).astype(held_as)


def setup_inputs(seed: int = 0, part: int = 0) -> dict:
    key_list = jax.random.split(jax.random.key(seed), 10)
    part_keys = jax.random.split(jax.random.fold_in(key_list[9], part), 10)
    attn = gaussian(part_keys[0], (ROWS, HA), 1.0, 6.0, ((0, 8), (1, 2)))
    o_weight = gaussian(key_list[1], (HA, D), HA ** -0.5, 0.09375, ((0, 2), (1, 2)))
    residual = draw_residual(jax.random.fold_in(jax.random.fold_in(key_list[9], part), 71), part)
    norm_gain = jnp.clip(1.0 + 0.18 * jax.random.normal(key_list[3], (D,), jnp.float32), 0.099609375, 1.8984375).astype(jnp.bfloat16)
    expert_ids_keys = jax.random.split(jax.random.fold_in(part_keys[4], 1), ROWS // ROWS_DEV)
    expert_ids_turns = jax.random.permutation(jax.random.fold_in(part_keys[4], 3), ROWS // ROWS_DEV)
    expert_ids = jax.vmap(lambda own, number: deal_out(jax.random.fold_in(part_keys[4], 2), own, number, ROWS_DEV, EXPERTS, TOPK, SLOT, 2))(expert_ids_keys, expert_ids_turns).reshape((ROWS, TOPK))
    route_weights = jnp.clip(jnp.exp(math.log(1.0) - 2.3025851 * jax.random.uniform(part_keys[5], (ROWS, TOPK), jnp.float32) ** level_of(part_keys[5], (ROWS, TOPK), ((0, 8),), -0.2, 0.2)), 0.1, 1.0)
    w_gate = gaussian(key_list[6], (EXPERTS, D, FF), D ** -0.5, 0.09375, ((0, 8), (2, 2)))
    w_up = gaussian(key_list[7], (EXPERTS, D, FF), D ** -0.5, 0.09375, ((0, 8), (2, 2)))
    w_down = bell_draw_with(key_list[8], (EXPERTS, FF, D), FF ** -0.5, 0.25, ((0, 8), (1, 2)), (1, 2, 2, 2.0))
    return {"attn": attn, "o_weight": o_weight, "residual": residual, "norm_gain": norm_gain, "expert_ids": expert_ids, "route_weights": route_weights, "w_gate": w_gate, "w_up": w_up, "w_down": w_down}


def run_expert(packed):
    slot_rows, gate_weight, up_weight, down_weight = packed
    gate_acc = jnp.dot(slot_rows, gate_weight, preferred_element_type=jnp.float32)
    up_acc = jnp.dot(slot_rows, up_weight, preferred_element_type=jnp.float32)
    activated = (jax.nn.silu(gate_acc) * up_acc).astype(jnp.bfloat16)
    total = jnp.zeros((slot_rows.shape[0], D), jnp.float32)
    for group in range(N_TENSOR):
        lower_edge = group * FF_PART
        piece_out = jnp.dot(activated[:, lower_edge:lower_edge + FF_PART], down_weight[lower_edge:lower_edge + FF_PART], preferred_element_type=jnp.float32).astype(jnp.bfloat16)
        piece_out = lax.optimization_barrier(piece_out)
        total = total + piece_out.astype(jnp.float32)
    return total.astype(jnp.bfloat16)

def reference(attn, o_weight, residual, norm_gain, expert_ids, route_weights, w_gate, w_up, w_down):
    summed = jnp.dot(attn, o_weight, preferred_element_type=jnp.float32) + residual.astype(jnp.float32)
    rounded = lax.optimization_barrier(summed.astype(jnp.bfloat16))
    hidden_f = rounded.astype(jnp.float32)
    mean_sq = lax.optimization_barrier(jnp.mean(hidden_f * hidden_f, axis=1, keepdims=True))
    normed = (hidden_f * lax.rsqrt(mean_sq + 1e-06) * norm_gain.astype(jnp.float32)).astype(jnp.bfloat16)
    block_count = ROWS // ROWS_DEV
    onehot = (expert_ids[:, :, None] == jnp.arange(EXPERTS, dtype=jnp.int32)).astype(jnp.int32)
    chosen = lax.optimization_barrier(jnp.sum(onehot, axis=1)).reshape(block_count, ROWS_DEV, EXPERTS)
    before = (jnp.cumsum(chosen, axis=1) - chosen).reshape(ROWS, EXPERTS)
    slot_index = lax.optimization_barrier(jnp.sum(onehot * before[:, None, :], axis=2)).astype(jnp.int32)
    block_index = jnp.broadcast_to((jnp.arange(ROWS, dtype=jnp.int32) // ROWS_DEV)[:, None], (ROWS, TOPK)).astype(jnp.int32)
    slots = jnp.zeros((EXPERTS, block_count, SLOT, D), jnp.bfloat16)
    slots = slots.at[expert_ids, block_index, slot_index].set(jnp.broadcast_to(normed[:, None, :], (ROWS, TOPK, D)))
    expert_out = lax.map(run_expert, (slots.reshape(EXPERTS, block_count * SLOT, D), w_gate, w_up, w_down))
    expert_out = expert_out.reshape(EXPERTS, block_count, SLOT, D)
    picked = expert_out[expert_ids, block_index, slot_index].astype(jnp.float32)
    moe_out = lax.optimization_barrier(jnp.sum(route_weights[:, :, None] * picked, axis=1))
    return moe_out.astype(jnp.bfloat16)
```

```python
import functools

import jax
import jax.numpy as jnp
from jax import lax
from jax.experimental import pallas as pl
from jax.experimental.pallas import tpu as pltpu
from jax.sharding import PartitionSpec as P

SLOT = 24

epsilon = 1e-06

CHUNKS = (4, 4)


def fetch(value, axis, step):
    size = lax.axis_size(axis)
    if step % size == 0:
        return value
    return lax.ppermute(value, axis, [((i + step) % size, i) for i in range(size)])


def pick(stacked, index):
    return lax.dynamic_index_in_dim(stacked, index, 0, keepdims=False)


def slot_codes(expert_ids, experts):
    rows_here = expert_ids.shape[0]
    onehot = (expert_ids[:, :, None] == jnp.arange(experts, dtype=jnp.int32)).astype(jnp.float32)
    chosen = jnp.sum(onehot, axis=1)
    row_ids = jnp.arange(rows_here)
    earlier = (row_ids[:, None] > row_ids[None, :]).astype(jnp.bfloat16)
    before = jnp.dot(
        earlier, chosen.astype(jnp.bfloat16), preferred_element_type=jnp.float32
    )
    slot = jnp.sum(onehot * before[:, None, :], axis=2)
    return expert_ids.astype(jnp.float32) * SLOT + slot


STEP = 512

F32, BF16 = jnp.float32, jnp.bfloat16
ANY = pl.BlockSpec(memory_space=pl.ANY)
VMEM = pl.BlockSpec(memory_space=pltpu.VMEM)
SMEM = pl.BlockSpec(memory_space=pltpu.SMEM)
PARAMS = pltpu.CompilerParams(vmem_limit_bytes=60 * 1024 * 1024)


def down_copies(sel_ref, wd_ref, wds_ref, sem_ref, first):
    tensors, held, _, span = wds_ref.shape
    copies = []
    for t in range(tensors):
        at = pl.multiple_of(sel_ref[t] + first, 128)
        for j in range(held):
            copies.append(
                pltpu.make_async_copy(
                    wd_ref.at[j, :, pl.ds(at, span)], wds_ref.at[t, j], sem_ref.at[t, j]
                )
            )
    return copies


def down_and_combine(sel_ref, back_ref, act_ref, wds_ref, outs_ref, mixed_ref, groups, tensors):
    held, slots, _ = act_ref.shape
    cores, _, group_slots = back_ref.shape
    span = wds_ref.shape[-1]
    step = min(STEP, span)
    per = slots // groups
    for t in range(tensors):

        @pl.loop(0, span // step)
        def _(n):
            cols = pl.ds(pl.multiple_of(n * step, step), step)
            for j in range(held):
                out = jnp.dot(act_ref[j], wds_ref[t, j, :, cols], preferred_element_type=F32)
                out = out.astype(BF16)
                for g in range(groups):
                    mixed_ref[g, j * per : (j + 1) * per, :] = out[g * per : (g + 1) * per]
            for i in range(cores):
                mixed = mixed_ref[i if groups > 1 else 0]
                rows = jnp.dot(back_ref[i], mixed, preferred_element_type=F32)
                outs_ref[i][t, :, cols] = rows.astype(BF16)


def first_kernel(
    dims, sel_ref, place_ref, back_ref, weight_ref, *rest
):
    cores, tensors, depth, groups, first = dims
    lengths = depth if groups > 1 else 1
    count = cores * tensors * lengths
    pieces, rest = rest[:count], rest[count:]
    wg_ref, wu_ref, wd_ref, act_ref = rest[:4]
    outs_ref = rest[4 : 4 + cores]
    x_ref, s_ref, wgs_ref, wus_ref, wds_ref, mixed_ref, x_sem, w_sem, d_sem = rest[4 + cores :]
    held = wg_ref.shape[0]
    part, cols = pieces[0].shape
    width = x_ref.shape[-1]
    copies = []
    for i in range(cores):
        at = pl.multiple_of(sel_ref[tensors + groups + i], 128)
        for k in range(tensors):
            for o in range(lengths):
                n = (i * tensors + k) * lengths + o
                g, row = (k, o) if groups > 1 else (0, k)
                copies.append(
                    pltpu.make_async_copy(
                        pieces[n],
                        x_ref.at[g, pl.ds(row * part, part), pl.ds(at, cols)],
                        x_sem.at[n],
                    )
                )
    for copy in copies:
        copy.start()
    weights = []
    for j in range(held):
        for n, (src, dst) in enumerate(((wg_ref, wgs_ref), (wu_ref, wus_ref))):
            weights.append(pltpu.make_async_copy(src.at[j], dst.at[j], w_sem.at[n, j]))
    for copy in weights:
        copy.start()
    downs = down_copies(sel_ref, wd_ref, wds_ref, d_sem, first)
    for copy in downs:
        copy.start()
    for copy in copies:
        copy.wait()

    per = s_ref.shape[1] // groups
    step = min(STEP, width)
    for g in range(groups):
        kk = sel_ref[tensors + g]

        @pl.loop(0, width // step)
        def _(n):
            at = pl.ds(pl.multiple_of(n * step, step), step)
            rows = jnp.dot(place_ref[g], x_ref[kk, :, at], preferred_element_type=F32)
            rows = rows.astype(BF16)
            for j in range(held):
                s_ref[j, g * per : (g + 1) * per, at] = rows[j * per : (j + 1) * per]

    @pl.loop(0, held)
    def _(j):
        pltpu.make_async_copy(wg_ref.at[j], wgs_ref.at[j], w_sem.at[0, j]).wait()
        gate = jnp.dot(s_ref[j], wgs_ref[j], preferred_element_type=F32)
        pltpu.make_async_copy(wu_ref.at[j], wus_ref.at[j], w_sem.at[1, j]).wait()
        up = jnp.dot(s_ref[j], wus_ref[j], preferred_element_type=F32)
        value = gate / (1.0 + jnp.exp(-gate)) * up * weight_ref[j]
        act_ref[j] = value.astype(BF16)

    for copy in downs:
        copy.wait()
    down_and_combine(sel_ref, back_ref, act_ref, wds_ref, outs_ref, mixed_ref, groups, tensors)


def later_kernel(dims, sel_ref, back_ref, act_ref, wd_ref, *rest):
    cores, tensors, groups, first = dims
    outs_ref = rest[:cores]
    wds_ref, mixed_ref, d_sem = rest[cores:]
    downs = down_copies(sel_ref, wd_ref, wds_ref, d_sem, first)
    for copy in downs:
        copy.start()
    for copy in downs:
        copy.wait()
    down_and_combine(sel_ref, back_ref, act_ref, wds_ref, outs_ref, mixed_ref, groups, tensors)


def on_device(attn, o_weight, residual, norm_gain, expert_ids, route_weights, w_gate, w_up, w_down):
    cores, tensors, depth = (lax.axis_size(a) for a in ("dp", "tensor", "expert"))
    d, x, z = (lax.axis_index(a) for a in ("dp", "tensor", "expert"))
    rows = attn.shape[0]
    width = norm_gain.shape[0]
    held, _, hidden_units = w_gate.shape
    experts = held * depth * cores
    sub = tensors // cores
    part = rows * cores // tensors
    cols_core = width // cores
    cols_out = width // tensors
    choices = expert_ids.shape[1]

    attn_all = jnp.concatenate([fetch(attn, "dp", i) for i in range(cores)], axis=0)
    res_all = jnp.concatenate([fetch(residual, "dp", i) for i in range(cores)], axis=0)
    partial = jnp.dot(attn_all, o_weight, preferred_element_type=F32)
    res_here = jnp.where(x // sub == d, res_all.astype(F32), 0.0)
    if sub == 1:
        partial = partial + res_here
    else:
        at = (x % sub) * cols_out
        partial = lax.dynamic_update_slice_in_dim(
            partial, lax.dynamic_slice_in_dim(partial, at, cols_out, 1) + res_here, at, 1
        )
    parts = partial.reshape(tensors, part, cols_core)

    def place(p):
        return ((p // sub - d) % cores) * sub + p % sub

    hidden = pick(parts, place(x))
    for k in range(1, tensors):
        sent = pick(parts, place((x - k) % tensors)).astype(BF16)
        hidden = hidden + fetch(sent, "tensor", k).astype(F32)
    hidden = hidden.astype(BF16).astype(F32)
    squares = jnp.sum(hidden * hidden, axis=1, keepdims=True)
    total = squares
    for i in range(1, cores):
        total = total + fetch(squares, "dp", i)
    inverse = lax.rsqrt(total / width + epsilon)
    gain = lax.dynamic_slice_in_dim(norm_gain, d * cols_core, cols_core, 0)
    normed = (hidden * inverse * gain.astype(F32)[None, :]).astype(BF16)

    codes = slot_codes(expert_ids, experts)
    route = jnp.concatenate([codes.T, route_weights.T], axis=0)
    normed, route = lax.optimization_barrier((normed, route))

    along = [fetch(normed, "expert", o) for o in range(depth)]
    if sub > 1:
        along = [jnp.concatenate(along, axis=0)]
    mine = [fetch(v, "tensor", k) for k in range(tensors) for v in along]
    pieces = [fetch(v, "dp", i) for i in range(cores) for v in mine]

    route = jnp.stack([fetch(route, "dp", i) for i in range(cores)])
    route = jnp.stack([fetch(route, "expert", o) for o in range(depth)])
    groups = tensors if sub == 1 else 1
    blocks = depth * cores // groups
    group_slots = held * blocks * SLOT
    local = route[:, :, :choices] - ((z * cores + d) * held * SLOT).astype(F32)
    valid = (local >= 0) & (local < held * SLOT)
    which = jnp.floor(local / SLOT)
    block_ids = jnp.arange(depth, dtype=F32)[:, None, None, None]
    if groups == 1:
        block_ids = block_ids * cores + jnp.arange(cores, dtype=F32)[None, :, None, None]
    slot = which * (blocks * SLOT) + block_ids * SLOT + (local - which * SLOT)
    slot = jnp.where(valid, slot, -1.0)
    weights = route[:, :, choices:]
    by_core = slot.transpose(1, 2, 0, 3).reshape(cores, choices, depth * rows)
    slot_ids = jnp.arange(group_slots, dtype=F32)
    back = jnp.any(by_core[..., None] == slot_ids, axis=1).astype(BF16)
    if groups > 1:
        table = jnp.concatenate([slot, weights], axis=2)
        table = table.transpose(1, 2, 0, 3).reshape(groups, 2 * choices, depth * rows)
    else:
        table = jnp.concatenate([slot, weights], axis=2)
        table = table.reshape(depth, cores, 2 * choices, sub, part)
        table = table.transpose(1, 3, 2, 0, 4).reshape(tensors, 2 * choices, depth * part)
        table = jnp.stack([pick(table, place((x + k) % tensors)) for k in range(tensors)])
        table = table.transpose(1, 0, 2).reshape(1, 2 * choices, -1)
    hit = table[:, :choices, None, :] == slot_ids[None, None, :, None]
    placing = jnp.any(hit, axis=1).astype(BF16)
    slot_weight = jnp.sum(jnp.where(hit, table[:, choices:, None, :], 0.0), axis=(1, 3))
    slot_weight = slot_weight.reshape(groups, held, blocks * SLOT).transpose(1, 0, 2)
    slot_weight = slot_weight.reshape(held, groups * blocks * SLOT, 1)

    starts = [((x + t) % tensors) * cols_out for t in range(tensors)]
    starts += [(d + g - x) % tensors if groups > 1 else d * 0 for g in range(groups)]
    starts += [((d + i) % cores) * cols_core for i in range(cores)]
    sel = jnp.stack(starts).astype(jnp.int32)

    slots = groups * blocks * SLOT
    spans = [cols_out * n // 8 for n in CHUNKS]
    out_rows = depth * rows

    def out_shapes(span):
        return [jax.ShapeDtypeStruct((tensors, out_rows, span), BF16)] * cores

    def scratch(span):
        return [
            pltpu.VMEM((tensors, held, hidden_units, span), BF16),
            pltpu.VMEM((groups, group_slots, min(STEP, span)), BF16),
        ]

    activated, *outs = pl.pallas_call(
        functools.partial(first_kernel, (cores, tensors, depth, groups, 0)),
        out_shape=[jax.ShapeDtypeStruct((held, slots, hidden_units), BF16)] + out_shapes(spans[0]),
        in_specs=[SMEM, VMEM, VMEM, VMEM] + [ANY] * (len(pieces) + 3),
        out_specs=[VMEM] * (1 + cores),
        scratch_shapes=[
            pltpu.VMEM((groups, tensors // groups * depth * part, width), BF16),
            pltpu.VMEM((held, slots, width), BF16),
            pltpu.VMEM(w_gate.shape, BF16),
            pltpu.VMEM(w_up.shape, BF16),
        ]
        + scratch(spans[0])
        + [
            pltpu.SemaphoreType.DMA((len(pieces),)),
            pltpu.SemaphoreType.DMA((2, held)),
            pltpu.SemaphoreType.DMA((tensors, held)),
        ],
        compiler_params=PARAMS,
        name="experts_first",
    )(sel, placing, back, slot_weight, *pieces, w_gate, w_up, w_down)

    results = []
    at = 0
    for n, span in enumerate(spans):
        if n > 0:
            outs = pl.pallas_call(
                functools.partial(later_kernel, (cores, tensors, groups, at)),
                out_shape=out_shapes(span),
                in_specs=[SMEM, VMEM, VMEM, ANY],
                out_specs=[VMEM] * cores,
                scratch_shapes=scratch(span) + [pltpu.SemaphoreType.DMA((tensors, held))],
                compiler_params=PARAMS,
                cost_estimate=pl.CostEstimate(
                    flops=4 * slots * held * hidden_units * span * tensors,
                    bytes_accessed=2 * held * hidden_units * span * tensors,
                    transcendentals=0,
                ),
                name="experts_later",
            )(sel, back, activated, w_down)
        at += span
        summed = outs[0].astype(F32)
        for i in range(1, cores):
            summed = summed + fetch(outs[i], "dp", -i).astype(F32)
        narrow = summed[0]
        for t in range(1, tensors):
            narrow = narrow + fetch(summed[t].astype(BF16), "tensor", -t).astype(F32)
        narrow = narrow.reshape(depth, rows, span)
        result = narrow[0]
        for o in range(1, depth):
            result = result + fetch(narrow[o].astype(BF16), "expert", -o).astype(F32)
        results.append(result.astype(BF16))
    return jnp.concatenate(results, axis=1)


def solution(mesh):
    placed = (
        P(("groups", "expert", "dp"), "tensor"),
        P("tensor", "dp"),
        P(("groups", "expert", "dp"), "tensor"),
        P(),
        P(("groups", "expert", "dp"), None),
        P(("groups", "expert", "dp"), None),
        P(("expert", "dp"), None, "tensor"),
        P(("expert", "dp"), None, "tensor"),
        P(("expert", "dp"), "tensor", None),
    )
    return jax.shard_map(
        on_device,
        mesh=mesh,
        in_specs=placed,
        out_specs=P(("groups", "expert", "dp"), "tensor"),
        check_vma=False,
    )
```

```python
import functools

import jax
import jax.numpy as jnp
from jax import lax
from jax.experimental import pallas as pl
from jax.experimental.pallas import tpu as pltpu
from jax.sharding import PartitionSpec as P


SLOT = 24

epsilon = 1e-06

CHUNKS = (4, 4)


def fetch(value, axis, step):
    size = lax.axis_size(axis)
    if step % size == 0:
        return value
    return lax.ppermute(value, axis, [((i + step) % size, i) for i in range(size)])


def across(value, axis, flip):
    size = lax.axis_size(axis)
    return lax.ppermute(value, axis, [(i ^ flip, i) for i in range(size)])


def pick(stacked, index):
    return lax.dynamic_index_in_dim(stacked, index, 0, keepdims=False)


def slot_codes(expert_ids, experts):
    rows_here = expert_ids.shape[0]
    onehot = (expert_ids[:, :, None] == jnp.arange(experts, dtype=jnp.int32)).astype(jnp.float32)
    chosen = jnp.sum(onehot, axis=1)
    row_ids = jnp.arange(rows_here)
    earlier = (row_ids[:, None] > row_ids[None, :]).astype(jnp.bfloat16)
    before = jnp.dot(
        earlier, chosen.astype(jnp.bfloat16), preferred_element_type=jnp.float32
    )
    slot = jnp.sum(onehot * before[:, None, :], axis=2)
    return expert_ids.astype(jnp.float32) * SLOT + slot


STEP = 1024

F32, BF16 = jnp.float32, jnp.bfloat16
ANY = pl.BlockSpec(memory_space=pl.ANY)
VMEM = pl.BlockSpec(memory_space=pltpu.VMEM)
SMEM = pl.BlockSpec(memory_space=pltpu.SMEM)
PARAMS = pltpu.CompilerParams(vmem_limit_bytes=60 * 1024 * 1024)


def down_copies(sel_ref, wd_ref, wds_ref, sem_ref, first):
    tensors, held, _, span = wds_ref.shape
    copies = [[] for _ in range(tensors)]
    for t in range(tensors):
        at = pl.multiple_of(sel_ref[t] + first, 128)
        for j in range(held):
            copies[t].append(
                pltpu.make_async_copy(
                    wd_ref.at[j, :, pl.ds(at, span)], wds_ref.at[t, j], sem_ref.at[t, j]
                )
            )
    return copies


def down_and_combine(back_ref, act_ref, wds_ref, outs_ref, mixed_ref, groups, waits):
    held, slots, _ = act_ref.shape
    cores, _, _ = back_ref.shape
    tensors, _, _, span = wds_ref.shape
    step = min(STEP, span)
    per = slots // groups
    for t in range(tensors):
        for copy in waits[t]:
            copy.wait()
        for n in range(span // step):
            cols = slice(n * step, (n + 1) * step)
            for j in range(held):
                out = jnp.dot(act_ref[j], wds_ref[t, j, :, cols], preferred_element_type=F32)
                out = out.astype(BF16)
                for g in range(groups):
                    mixed_ref[g, j * per : (j + 1) * per, :] = out[g * per : (g + 1) * per]
            for i in range(cores):
                mixed = mixed_ref[i if groups > 1 else 0]
                rows = jnp.dot(back_ref[i], mixed, preferred_element_type=F32)
                outs_ref[i][t, :, cols] = rows.astype(BF16)


def first_kernel(
    dims, sel_ref, place_ref, back_ref, *rest
):
    cores, tensors, depth, groups, first = dims
    lengths = depth if groups > 1 else 1
    count = cores * tensors * lengths
    pieces, rest = rest[:count], rest[count:]
    wg_ref, wu_ref, wd_ref, act_ref = rest[:4]
    outs_ref = rest[4 : 4 + cores]
    x_ref, s_ref, wgs_ref, wus_ref, wds_ref, mixed_ref, x_sem, w_sem, d_sem = rest[4 + cores :]
    held = wg_ref.shape[0]
    part, cols = pieces[0].shape
    width = x_ref.shape[-1]
    copies = []
    for i in range(cores):
        at = pl.multiple_of(sel_ref[tensors + groups + i], 128)
        for k in range(tensors):
            for o in range(lengths):
                n = (i * tensors + k) * lengths + o
                g, row = (k, o) if groups > 1 else (0, k)
                copies.append(
                    pltpu.make_async_copy(
                        pieces[n],
                        x_ref.at[g, pl.ds(row * part, part), pl.ds(at, cols)],
                        x_sem.at[n],
                    )
                )
    for copy in copies:
        copy.start()
    for copy in copies:
        copy.wait()

    def weights(j):
        return [
            pltpu.make_async_copy(src.at[j], dst.at[j], w_sem.at[n, j])
            for n, (src, dst) in enumerate(((wg_ref, wgs_ref), (wu_ref, wus_ref)))
        ]

    downs = down_copies(sel_ref, wd_ref, wds_ref, d_sem, first)
    queue = [weights(j) for j in range(held)] + downs

    def start(n):
        if n < len(queue):
            for copy in queue[n]:
                copy.start()

    start(0)
    per = s_ref.shape[1] // groups
    step = min(STEP, width)
    for g in range(groups):
        kk = sel_ref[tensors + g]
        for n in range(width // step):
            at = slice(n * step, (n + 1) * step)
            rows = jnp.dot(place_ref[g], x_ref[kk, :, at], preferred_element_type=F32)
            rows = rows.astype(BF16)
            for j in range(held):
                s_ref[j, g * per : (g + 1) * per, at] = rows[j * per : (j + 1) * per]
        if g == 0:
            start(1)

    for j in range(held):
        start(j + 2)
        wait_gate, wait_up = weights(j)
        wait_gate.wait()
        gate = jnp.dot(s_ref[j], wgs_ref[j], preferred_element_type=F32)
        wait_up.wait()
        up = jnp.dot(s_ref[j], wus_ref[j], preferred_element_type=F32)
        act_ref[j] = (gate / (1.0 + jnp.exp(-gate)) * up).astype(BF16)
    for n in range(held + 2, len(queue)):
        start(n)
    down_and_combine(back_ref, act_ref, wds_ref, outs_ref, mixed_ref, groups, downs)


def later_kernel(dims, sel_ref, back_ref, act_ref, wd_ref, *rest):
    cores, _, groups, first = dims
    outs_ref = rest[:cores]
    wds_ref, mixed_ref, d_sem = rest[cores:]
    downs = down_copies(sel_ref, wd_ref, wds_ref, d_sem, first)
    for copies in downs:
        for copy in copies:
            copy.start()
    down_and_combine(back_ref, act_ref, wds_ref, outs_ref, mixed_ref, groups, downs)


def on_device(attn, o_weight, residual, norm_gain, expert_ids, route_weights, w_gate, w_up, w_down):
    cores, tensors, depth = (lax.axis_size(a) for a in ("dp", "tensor", "expert"))
    d, x, z = (lax.axis_index(a) for a in ("dp", "tensor", "expert"))
    rows = attn.shape[0]
    width = norm_gain.shape[0]
    held, _, hidden_units = w_gate.shape
    experts = held * depth * cores
    sub = tensors // cores
    part = rows * cores // tensors
    cols_core = width // cores
    cols_out = width // tensors
    choices = expert_ids.shape[1]

    attn_all = jnp.concatenate([fetch(attn, "dp", i) for i in range(cores)], axis=0)
    res_all = jnp.concatenate([fetch(residual, "dp", i) for i in range(cores)], axis=0)
    partial = jnp.dot(attn_all, o_weight, preferred_element_type=F32)
    res_here = jnp.where(x // sub == d, res_all.astype(F32), 0.0)
    if sub == 1:
        partial = partial + res_here
    else:
        at = (x % sub) * cols_out
        partial = lax.dynamic_update_slice_in_dim(
            partial, lax.dynamic_slice_in_dim(partial, at, cols_out, 1) + res_here, at, 1
        )
    parts = partial.reshape(tensors, part, cols_core)

    def place(p):
        return ((p // sub - d) % cores) * sub + p % sub

    hidden = pick(parts, place(x))
    for k in range(1, tensors):
        sent = pick(parts, place((x - k) % tensors)).astype(BF16)
        hidden = hidden + fetch(sent, "tensor", k).astype(F32)
    hidden = hidden.astype(BF16).astype(F32)
    squares = jnp.sum(hidden * hidden, axis=1, keepdims=True)
    total = squares
    for i in range(1, cores):
        total = total + fetch(squares, "dp", i)
    inverse = lax.rsqrt(total / width + epsilon)
    gain = lax.dynamic_slice_in_dim(norm_gain, d * cols_core, cols_core, 0)
    normed = (hidden * inverse * gain.astype(F32)[None, :]).astype(BF16)

    codes = slot_codes(expert_ids, experts)
    route = jnp.concatenate([codes.T, route_weights.T], axis=0)
    route = jnp.stack([fetch(route, "dp", i) for i in range(cores)])
    routes = [route]
    for o in range(1, depth):
        routes.append(across(route, "expert", o))
    route = jnp.stack(routes)
    groups = tensors if sub == 1 else 1
    blocks = depth * cores // groups
    group_slots = held * blocks * SLOT
    local = route[:, :, :choices] - ((z * cores + d) * held * SLOT).astype(F32)
    valid = (local >= 0) & (local < held * SLOT)
    which = jnp.floor(local / SLOT)
    block_ids = jnp.arange(depth, dtype=F32)[:, None, None, None]
    if groups == 1:
        block_ids = block_ids * cores + jnp.arange(cores, dtype=F32)[None, :, None, None]
    slot = which * (blocks * SLOT) + block_ids * SLOT + (local - which * SLOT)
    slot = jnp.where(valid, slot, -1.0)
    weights = route[:, :, choices:]
    by_core = slot.transpose(1, 2, 0, 3).reshape(cores, choices, depth * rows, 1)
    weight_by_core = weights.transpose(1, 2, 0, 3).reshape(cores, choices, depth * rows, 1)
    slot_ids = jnp.arange(group_slots, dtype=F32)
    back = jnp.sum(jnp.where(by_core == slot_ids, weight_by_core, 0.0), axis=1).astype(BF16)
    if groups > 1:
        table = slot.transpose(1, 2, 0, 3).reshape(groups, choices, depth * rows)
    else:
        table = slot.reshape(depth, cores, choices, sub, part)
        table = table.transpose(1, 3, 2, 0, 4).reshape(tensors, choices, depth * part)
        table = jnp.stack([pick(table, place((x + k) % tensors)) for k in range(tensors)])
        table = table.transpose(1, 0, 2).reshape(1, choices, -1)
    placing = jnp.any(table[:, :, None, :] == slot_ids[:, None], axis=1).astype(BF16)

    along = [normed]
    mine = {}
    for o in range(depth):
        if o > 0:
            along.append(across(along[o & (o - 1)], "expert", o & -o))
    if sub > 1:
        along = [jnp.concatenate(along, axis=0)]
    else:
        held_back = lax.optimization_barrier((along[-1], placing, back))
        along[-1], placing, back = held_back
    for o, value in enumerate(along):
        for k in range(tensors):
            mine[k, o] = fetch(value, "tensor", k)
    pieces = []
    for i in range(cores):
        for k in range(tensors):
            for o in range(len(along)):
                pieces.append(fetch(mine[k, o], "dp", i))

    starts = [((x + t) % tensors) * cols_out for t in range(tensors)]
    starts += [(d + g - x) % tensors if groups > 1 else d * 0 for g in range(groups)]
    starts += [((d + i) % cores) * cols_core for i in range(cores)]
    sel = jnp.stack(starts).astype(jnp.int32)

    slots = groups * blocks * SLOT
    spans = [cols_out * n // 8 for n in CHUNKS]
    out_rows = depth * rows

    def out_shapes(span):
        return [jax.ShapeDtypeStruct((tensors, out_rows, span), BF16)] * cores

    def scratch(span):
        return [
            pltpu.VMEM((tensors, held, hidden_units, span), BF16),
            pltpu.VMEM((groups, group_slots, min(STEP, span)), BF16),
        ]

    activated, *outs = pl.pallas_call(
        functools.partial(first_kernel, (cores, tensors, depth, groups, 0)),
        out_shape=[jax.ShapeDtypeStruct((held, slots, hidden_units), BF16)] + out_shapes(spans[0]),
        in_specs=[SMEM, VMEM, VMEM] + [ANY] * (len(pieces) + 3),
        out_specs=[VMEM] * (1 + cores),
        scratch_shapes=[
            pltpu.VMEM((groups, tensors // groups * depth * part, width), BF16),
            pltpu.VMEM((held, slots, width), BF16),
            pltpu.VMEM(w_gate.shape, BF16),
            pltpu.VMEM(w_up.shape, BF16),
        ]
        + scratch(spans[0])
        + [
            pltpu.SemaphoreType.DMA((len(pieces),)),
            pltpu.SemaphoreType.DMA((2, held)),
            pltpu.SemaphoreType.DMA((tensors, held)),
        ],
        compiler_params=PARAMS,
        name="experts_first",
    )(sel, placing, back, *pieces, w_gate, w_up, w_down)

    results = []
    at = 0
    for n, span in enumerate(spans):
        if n > 0:
            outs = pl.pallas_call(
                functools.partial(later_kernel, (cores, tensors, groups, at)),
                out_shape=out_shapes(span),
                in_specs=[SMEM, VMEM, VMEM, ANY],
                out_specs=[VMEM] * cores,
                scratch_shapes=scratch(span) + [pltpu.SemaphoreType.DMA((tensors, held))],
                compiler_params=PARAMS,
                cost_estimate=pl.CostEstimate(
                    flops=4 * slots * held * hidden_units * span * tensors,
                    bytes_accessed=2 * held * hidden_units * span * tensors,
                    transcendentals=0,
                ),
                name="experts_later",
            )(sel, back, activated, w_down)
        at += span
        summed = outs[0].astype(F32)
        for i in range(1, cores):
            got = fetch(outs[i], "dp", -i)
            summed = summed + got.astype(F32)
        narrow = summed[0]
        for t in range(1, tensors):
            got = fetch(summed[t].astype(BF16), "tensor", -t)
            narrow = narrow + got.astype(F32)
        narrow = narrow.reshape(depth, rows, span)
        flip = 1
        while flip < depth:
            narrow = narrow.reshape(-1, 2, rows, span)
            got = across(narrow[:, 1].astype(BF16), "expert", flip)
            narrow = narrow[:, 0] + got.astype(F32)
            flip *= 2
        results.append(narrow[0].astype(BF16))
    return jnp.concatenate(results, axis=1)


def solution(mesh):
    placed = (
        P(("groups", "expert", "dp"), "tensor"),
        P("tensor", "dp"),
        P(("groups", "expert", "dp"), "tensor"),
        P(),
        P(("groups", "expert", "dp"), None),
        P(("groups", "expert", "dp"), None),
        P(("expert", "dp"), None, "tensor"),
        P(("expert", "dp"), None, "tensor"),
        P(("expert", "dp"), "tensor", None),
    )

    step = jax.shard_map(
        on_device,
        mesh=mesh,
        in_specs=placed,
        out_specs=P(("groups", "expert", "dp"), "tensor"),
        check_vma=False,
    )
    if mesh.shape["tensor"] != mesh.shape["dp"]:
        return step
    return step
```

```python
import functools

import jax
import jax.numpy as jnp
from jax import lax
from jax.experimental import pallas as pl
from jax.experimental.pallas import tpu as pltpu
from jax.sharding import PartitionSpec as P


SLOT = 24

epsilon = 1e-06

CHUNKS = (4, 3, 1)


def fetch(value, axis, step):
    size = lax.axis_size(axis)
    if step % size == 0:
        return value
    return lax.ppermute(value, axis, [((i + step) % size, i) for i in range(size)])


def across(value, axis, flip):
    size = lax.axis_size(axis)
    return lax.ppermute(value, axis, [(i ^ flip, i) for i in range(size)])


def pick(stacked, index):
    return lax.dynamic_index_in_dim(stacked, index, 0, keepdims=False)


STEP = 1024

F32, BF16 = jnp.float32, jnp.bfloat16
ANY = pl.BlockSpec(memory_space=pl.ANY)
VMEM = pl.BlockSpec(memory_space=pltpu.VMEM)
SMEM = pl.BlockSpec(memory_space=pltpu.SMEM)
SMALL = pltpu.CompilerParams(vmem_limit_bytes=8 * 1024 * 1024)
PARAMS = pltpu.CompilerParams(vmem_limit_bytes=60 * 1024 * 1024)


def codes_kernel(experts, ids_ref, weights_ref, out_ref):
    rows, choices = ids_ref.shape
    ids = ids_ref[...]
    lanes = lax.broadcasted_iota(jnp.int32, (rows, experts), 1)
    picked = [(ids[:, k : k + 1] == lanes).astype(F32) for k in range(choices)]
    chosen = functools.reduce(jnp.add, picked)
    earlier = lax.broadcasted_iota(jnp.int32, (rows, rows), 0) > lax.broadcasted_iota(
        jnp.int32, (rows, rows), 1
    )
    before = jnp.dot(
        earlier.astype(F32).astype(BF16), chosen.astype(BF16), preferred_element_type=F32
    )
    slot = [jnp.sum(p * before, axis=1, keepdims=True) for p in picked]
    codes = jnp.concatenate(slot, axis=1) + ids.astype(F32) * SLOT
    out_ref[...] = jnp.concatenate([codes, weights_ref[...]], axis=1).T


def tables_kernel(choices, base_ref, *rest):
    routes, (place_ref, back_ref) = rest[:-2], rest[-2:]
    depth = len(routes)
    cores, group_slots, out_rows = place_ref.shape
    per = depth * SLOT
    base = base_ref[0].astype(F32)
    for i in range(cores):
        slots = []
        for o in range(depth):
            local = routes[o][i, :choices] - base
            which = jnp.floor((local + 0.5) * (1.0 / SLOT))
            slot = which * (per - SLOT) + local + o * SLOT
            slots.append(jnp.where((local >= 0) & (local < group_slots // depth), slot, -1.0))
        slot = jnp.concatenate(slots, axis=1).astype(jnp.int32)
        down = lax.broadcasted_iota(jnp.int32, (group_slots, out_rows), 0)
        hit = [slot[k : k + 1] == down for k in range(choices)]
        place_ref[i] = functools.reduce(jnp.logical_or, hit).astype(F32).astype(BF16)
        turned = slot.astype(F32).T.astype(jnp.int32)
        weights = jnp.concatenate([routes[o][i, choices:] for o in range(depth)], axis=1).T
        along = lax.broadcasted_iota(jnp.int32, (out_rows, group_slots), 1)
        total = jnp.zeros((out_rows, group_slots), F32)
        for k in range(choices):
            total = jnp.where(turned[:, k : k + 1] == along, weights[:, k : k + 1], total)
        back_ref[i] = total.astype(BF16)


def down_copies(sel_ref, wd_ref, wds_ref, sem_ref, first):
    tensors, held, _, span = wds_ref.shape
    copies = [[] for _ in range(tensors)]
    for t in range(tensors):
        at = pl.multiple_of(sel_ref[t] + first, 128)
        for j in range(held):
            copies[t].append(
                pltpu.make_async_copy(
                    wd_ref.at[j, :, pl.ds(at, span)], wds_ref.at[t, j], sem_ref.at[t, j]
                )
            )
    return copies


def down_and_combine(back_ref, act_ref, wds_ref, outs_ref, mixed_ref, groups, waits):
    held, slots, _ = act_ref.shape
    cores, _, _ = back_ref.shape
    tensors, _, _, span = wds_ref.shape
    step = min(STEP, span)
    per = slots // groups
    for t in range(tensors):
        for copy in waits[t]:
            copy.wait()
        for n in range(span // step):
            cols = slice(n * step, (n + 1) * step)
            for j in range(held):
                out = jnp.dot(act_ref[j], wds_ref[t, j, :, cols], preferred_element_type=F32)
                out = out.astype(BF16)
                for g in range(groups):
                    mixed_ref[g, j * per : (j + 1) * per, :] = out[g * per : (g + 1) * per]
            for i in range(cores):
                mixed = mixed_ref[i if groups > 1 else 0]
                rows = jnp.dot(back_ref[i], mixed, preferred_element_type=F32)
                outs_ref[i][t, :, cols] = rows.astype(BF16)


def first_kernel(
    dims, sel_ref, place_ref, back_ref, *rest
):
    cores, tensors, depth, groups, first = dims
    lengths = depth if groups > 1 else 1
    count = cores * tensors * lengths
    pieces, rest = rest[:count], rest[count:]
    wg_ref, wu_ref, wd_ref, act_ref = rest[:4]
    outs_ref = rest[4 : 4 + cores]
    x_ref, s_ref, wgs_ref, wus_ref, wds_ref, mixed_ref, x_sem, w_sem, d_sem = rest[4 + cores :]
    held = wg_ref.shape[0]
    part, cols = pieces[0].shape
    width = x_ref.shape[-1]
    copies = []
    for i in range(cores):
        at = pl.multiple_of(sel_ref[tensors + groups + i], 128)
        for k in range(tensors):
            for o in range(lengths):
                n = (i * tensors + k) * lengths + o
                g, row = (k, o) if groups > 1 else (0, k)
                copies.append(
                    pltpu.make_async_copy(
                        pieces[n],
                        x_ref.at[g, pl.ds(row * part, part), pl.ds(at, cols)],
                        x_sem.at[n],
                    )
                )
    for copy in copies:
        copy.start()
    for copy in copies:
        copy.wait()

    def weights(j):
        return [
            pltpu.make_async_copy(src.at[j], dst.at[j], w_sem.at[n, j])
            for n, (src, dst) in enumerate(((wg_ref, wgs_ref), (wu_ref, wus_ref)))
        ]

    downs = down_copies(sel_ref, wd_ref, wds_ref, d_sem, first)
    queue = [weights(j) for j in range(held)] + downs

    def start(n):
        if n < len(queue):
            for copy in queue[n]:
                copy.start()

    start(0)
    per = s_ref.shape[1] // groups
    step = min(STEP, width)
    for g in range(groups):
        kk = sel_ref[tensors + g]
        for n in range(width // step):
            at = slice(n * step, (n + 1) * step)
            rows = jnp.dot(place_ref[g], x_ref[kk, :, at], preferred_element_type=F32)
            rows = rows.astype(BF16)
            for j in range(held):
                s_ref[j, g * per : (g + 1) * per, at] = rows[j * per : (j + 1) * per]
        if g == 0:
            start(1)

    for j in range(held):
        start(j + 2)
        wait_gate, wait_up = weights(j)
        wait_gate.wait()
        gate = jnp.dot(s_ref[j], wgs_ref[j], preferred_element_type=F32)
        wait_up.wait()
        up = jnp.dot(s_ref[j], wus_ref[j], preferred_element_type=F32)
        act_ref[j] = (gate / (1.0 + jnp.exp(-gate)) * up).astype(BF16)
    for n in range(held + 2, len(queue)):
        start(n)
    down_and_combine(back_ref, act_ref, wds_ref, outs_ref, mixed_ref, groups, downs)


def later_kernel(dims, sel_ref, back_ref, act_ref, wd_ref, *rest):
    cores, _, groups, first = dims
    outs_ref = rest[:cores]
    wds_ref, mixed_ref, d_sem = rest[cores:]
    downs = down_copies(sel_ref, wd_ref, wds_ref, d_sem, first)
    for copies in downs:
        for copy in copies:
            copy.start()
    down_and_combine(back_ref, act_ref, wds_ref, outs_ref, mixed_ref, groups, downs)


def on_device(attn, o_weight, residual, norm_gain, expert_ids, route_weights, w_gate, w_up, w_down):
    cores, tensors, depth = (lax.axis_size(a) for a in ("dp", "tensor", "expert"))
    d, x, z = (lax.axis_index(a) for a in ("dp", "tensor", "expert"))
    rows = attn.shape[0]
    width = norm_gain.shape[0]
    held, _, hidden_units = w_gate.shape
    experts = held * depth * cores
    sub = tensors // cores
    part = rows * cores // tensors
    cols_core = width // cores
    cols_out = width // tensors
    choices = expert_ids.shape[1]

    attn_all = jnp.concatenate([fetch(attn, "dp", i) for i in range(cores)], axis=0)
    res_all = jnp.concatenate([fetch(residual, "dp", i) for i in range(cores)], axis=0)
    partial = jnp.dot(attn_all, o_weight, preferred_element_type=F32)
    res_here = jnp.where(x // sub == d, res_all.astype(F32), 0.0)
    if sub == 1:
        partial = partial + res_here
    else:
        at = (x % sub) * cols_out
        partial = lax.dynamic_update_slice_in_dim(
            partial, lax.dynamic_slice_in_dim(partial, at, cols_out, 1) + res_here, at, 1
        )
    parts = partial.reshape(tensors, part, cols_core)

    def place(p):
        return ((p // sub - d) % cores) * sub + p % sub

    hidden = pick(parts, place(x))
    for k in range(1, tensors):
        sent = pick(parts, place((x - k) % tensors)).astype(BF16)
        hidden = hidden + fetch(sent, "tensor", k).astype(F32)
    hidden = hidden.astype(BF16).astype(F32)
    squares = jnp.sum(hidden * hidden, axis=1, keepdims=True)
    total = squares
    for i in range(1, cores):
        total = total + fetch(squares, "dp", i)
    inverse = lax.rsqrt(total / width + epsilon)
    gain = lax.dynamic_slice_in_dim(norm_gain, d * cols_core, cols_core, 0)
    normed = (hidden * inverse * gain.astype(F32)[None, :]).astype(BF16)

    route = pl.pallas_call(
        functools.partial(codes_kernel, experts),
        out_shape=jax.ShapeDtypeStruct((2 * choices, rows), F32),
        in_specs=[VMEM, VMEM],
        out_specs=VMEM,
        compiler_params=SMALL,
        name="codes",
    )(expert_ids, route_weights)
    route = jnp.stack([fetch(route, "dp", i) for i in range(cores)])
    routes = [route]
    for o in range(1, depth):
        routes.append(across(route, "expert", o))
    groups = tensors if sub == 1 else 1
    blocks = depth * cores // groups
    group_slots = held * blocks * SLOT
    first_code = (z * cores + d) * held * SLOT
    if groups > 1:
        placing, back = pl.pallas_call(
            functools.partial(tables_kernel, choices),
            out_shape=[
                jax.ShapeDtypeStruct((cores, group_slots, depth * rows), BF16),
                jax.ShapeDtypeStruct((cores, depth * rows, group_slots), BF16),
            ],
            in_specs=[SMEM] + [VMEM] * depth,
            out_specs=[VMEM, VMEM],
            compiler_params=SMALL,
            name="tables",
        )(first_code.astype(jnp.int32).reshape(1), *routes)
    else:
        route = jnp.stack(routes)
        local = route[:, :, :choices] - first_code.astype(F32)
        valid = (local >= 0) & (local < held * SLOT)
        which = jnp.floor(local / SLOT)
        block_ids = jnp.arange(depth, dtype=F32)[:, None, None, None]
        block_ids = block_ids * cores + jnp.arange(cores, dtype=F32)[None, :, None, None]
        slot = which * (blocks * SLOT) + block_ids * SLOT + (local - which * SLOT)
        slot = jnp.where(valid, slot, -1.0)
        weights = route[:, :, choices:]
        by_core = slot.transpose(1, 2, 0, 3).reshape(cores, choices, depth * rows, 1)
        weight_by_core = weights.transpose(1, 2, 0, 3).reshape(cores, choices, depth * rows, 1)
        slot_ids = jnp.arange(group_slots, dtype=F32)
        back = jnp.sum(jnp.where(by_core == slot_ids, weight_by_core, 0.0), axis=1).astype(BF16)
        table = slot.reshape(depth, cores, choices, sub, part)
        table = table.transpose(1, 3, 2, 0, 4).reshape(tensors, choices, depth * part)
        table = jnp.stack([pick(table, place((x + k) % tensors)) for k in range(tensors)])
        table = table.transpose(1, 0, 2).reshape(1, choices, -1)
        placing = jnp.any(table[:, :, None, :] == slot_ids[:, None], axis=1).astype(BF16)

    along = [normed]
    mine = {}
    for o in range(depth):
        if o > 0:
            along.append(across(along[o & (o - 1)], "expert", o & -o))
    if sub > 1:
        along = [jnp.concatenate(along, axis=0)]
    for o, value in enumerate(along):
        for k in range(tensors):
            mine[k, o] = fetch(value, "tensor", k)
    pieces = []
    for i in range(cores):
        for k in range(tensors):
            for o in range(len(along)):
                pieces.append(fetch(mine[k, o], "dp", i))

    starts = [((x + t) % tensors) * cols_out for t in range(tensors)]
    starts += [(d + g - x) % tensors if groups > 1 else d * 0 for g in range(groups)]
    starts += [((d + i) % cores) * cols_core for i in range(cores)]
    sel = jnp.stack(starts).astype(jnp.int32)

    slots = groups * blocks * SLOT
    spans = [cols_out * n // 8 for n in CHUNKS]
    out_rows = depth * rows

    def out_shapes(span):
        return [jax.ShapeDtypeStruct((tensors, out_rows, span), BF16)] * cores

    def scratch(span):
        return [
            pltpu.VMEM((tensors, held, hidden_units, span), BF16),
            pltpu.VMEM((groups, group_slots, min(STEP, span)), BF16),
        ]

    activated, *outs = pl.pallas_call(
        functools.partial(first_kernel, (cores, tensors, depth, groups, 0)),
        out_shape=[jax.ShapeDtypeStruct((held, slots, hidden_units), BF16)] + out_shapes(spans[0]),
        in_specs=[SMEM, VMEM, VMEM] + [ANY] * (len(pieces) + 3),
        out_specs=[VMEM] * (1 + cores),
        scratch_shapes=[
            pltpu.VMEM((groups, tensors // groups * depth * part, width), BF16),
            pltpu.VMEM((held, slots, width), BF16),
            pltpu.VMEM(w_gate.shape, BF16),
            pltpu.VMEM(w_up.shape, BF16),
        ]
        + scratch(spans[0])
        + [
            pltpu.SemaphoreType.DMA((len(pieces),)),
            pltpu.SemaphoreType.DMA((2, held)),
            pltpu.SemaphoreType.DMA((tensors, held)),
        ],
        compiler_params=PARAMS,
        name="experts_first",
    )(sel, placing, back, *pieces, w_gate, w_up, w_down)

    results = []
    at = 0
    for n, span in enumerate(spans):
        if n > 0:
            outs = pl.pallas_call(
                functools.partial(later_kernel, (cores, tensors, groups, at)),
                out_shape=out_shapes(span),
                in_specs=[SMEM, VMEM, VMEM, ANY],
                out_specs=[VMEM] * cores,
                scratch_shapes=scratch(span) + [pltpu.SemaphoreType.DMA((tensors, held))],
                compiler_params=PARAMS,
                cost_estimate=pl.CostEstimate(
                    flops=4 * slots * held * hidden_units * span * tensors,
                    bytes_accessed=2 * held * hidden_units * span * tensors,
                    transcendentals=0,
                ),
                name="experts_later",
            )(sel, back, activated, w_down)
        at += span
        sides = []
        for t in list(range(1, tensors)) + [0]:
            summed = outs[0][t].astype(F32)
            for i in range(1, cores):
                got = fetch(outs[i][t], "dp", -i)
                summed = summed + got.astype(F32)
            if t > 0:
                got = fetch(summed.astype(BF16), "tensor", -t)
                sides.append(got)
        narrow = summed
        for got in sides:
            narrow = narrow + got.astype(F32)
        narrow = narrow.reshape(depth, rows, span)
        flip = 1
        while flip < depth:
            narrow = narrow.reshape(-1, 2, rows, span)
            got = across(narrow[:, 1].astype(BF16), "expert", flip)
            narrow = narrow[:, 0] + got.astype(F32)
            flip *= 2
        results.append(narrow[0].astype(BF16))
    return jnp.concatenate(results, axis=1)


def solution(mesh):
    placed = (
        P(("groups", "expert", "dp"), "tensor"),
        P("tensor", "dp"),
        P(("groups", "expert", "dp"), "tensor"),
        P(),
        P(("groups", "expert", "dp"), None),
        P(("groups", "expert", "dp"), None),
        P(("expert", "dp"), None, "tensor"),
        P(("expert", "dp"), None, "tensor"),
        P(("expert", "dp"), "tensor", None),
    )

    step = jax.shard_map(
        on_device,
        mesh=mesh,
        in_specs=placed,
        out_specs=P(("groups", "expert", "dp"), "tensor"),
        check_vma=False,
    )
    if mesh.shape["tensor"] != mesh.shape["dp"]:
        return step
    return step
```

```python
import functools

import jax
import jax.numpy as jnp
from jax import lax
from jax.experimental import pallas as pl
from jax.experimental.pallas import tpu as pltpu
from jax.sharding import PartitionSpec as P


SLOT = 24

epsilon = 1e-06

CHUNKS = (4, 4)


def fetch(value, axis, step):
    size = lax.axis_size(axis)
    if step % size == 0:
        return value
    return lax.ppermute(value, axis, [((i + step) % size, i) for i in range(size)])


def across(value, axis, flip):
    size = lax.axis_size(axis)
    return lax.ppermute(value, axis, [(i ^ flip, i) for i in range(size)])


def pick(stacked, index):
    return lax.dynamic_index_in_dim(stacked, index, 0, keepdims=False)


STEP = 1024

F32, BF16 = jnp.float32, jnp.bfloat16
ANY = pl.BlockSpec(memory_space=pl.ANY)
VMEM = pl.BlockSpec(memory_space=pltpu.VMEM)
SMEM = pl.BlockSpec(memory_space=pltpu.SMEM)
SMALL = pltpu.CompilerParams(vmem_limit_bytes=8 * 1024 * 1024)
PARAMS = pltpu.CompilerParams(vmem_limit_bytes=60 * 1024 * 1024)


def codes_kernel(experts, ids_ref, weights_ref, out_ref):
    rows, choices = ids_ref.shape
    ids = ids_ref[...]
    lanes = lax.broadcasted_iota(jnp.int32, (rows, experts), 1)
    picked = [(ids[:, k : k + 1] == lanes).astype(F32) for k in range(choices)]
    chosen = functools.reduce(jnp.add, picked)
    earlier = lax.broadcasted_iota(jnp.int32, (rows, rows), 0) > lax.broadcasted_iota(
        jnp.int32, (rows, rows), 1
    )
    before = jnp.dot(
        earlier.astype(F32).astype(BF16), chosen.astype(BF16), preferred_element_type=F32
    )
    slot = [jnp.sum(p * before, axis=1, keepdims=True) for p in picked]
    codes = jnp.concatenate(slot, axis=1) + ids.astype(F32) * SLOT
    out_ref[...] = jnp.concatenate([codes, weights_ref[...]], axis=1).T


def tables_kernel(choices, base_ref, *rest):
    routes, (place_ref, back_ref) = rest[:-2], rest[-2:]
    depth = len(routes)
    cores, group_slots, out_rows = place_ref.shape
    per = depth * SLOT
    base = base_ref[0].astype(F32)
    for i in range(cores):
        slots = []
        for o in range(depth):
            local = routes[o][i, :choices] - base
            which = jnp.floor((local + 0.5) * (1.0 / SLOT))
            slot = which * (per - SLOT) + local + o * SLOT
            slots.append(jnp.where((local >= 0) & (local < group_slots // depth), slot, -1.0))
        slot = jnp.concatenate(slots, axis=1).astype(jnp.int32)
        down = lax.broadcasted_iota(jnp.int32, (group_slots, out_rows), 0)
        hit = [slot[k : k + 1] == down for k in range(choices)]
        place_ref[i] = functools.reduce(jnp.logical_or, hit).astype(F32).astype(BF16)
        turned = slot.astype(F32).T.astype(jnp.int32)
        weights = jnp.concatenate([routes[o][i, choices:] for o in range(depth)], axis=1).T
        along = lax.broadcasted_iota(jnp.int32, (out_rows, group_slots), 1)
        total = jnp.zeros((out_rows, group_slots), F32)
        for k in range(choices):
            total = jnp.where(turned[:, k : k + 1] == along, weights[:, k : k + 1], total)
        back_ref[i] = total.astype(BF16)


def down_copies(wd_ref, wds_ref, sem_ref, first):
    tensors, held, _, span = wds_ref.shape
    x = lax.axis_index("tensor")
    cols_out = wd_ref.shape[2] // tensors
    copies = [[] for _ in range(tensors)]
    for t in range(tensors):
        at = pl.multiple_of((x + t) % tensors * cols_out + first, 128)
        for j in range(held):
            copies[t].append(
                pltpu.make_async_copy(
                    wd_ref.at[j, :, pl.ds(at, span)], wds_ref.at[t, j], sem_ref.at[t, j]
                )
            )
    return copies


def down_and_combine(back_ref, act_ref, wds_ref, outs_ref, mixed_ref, groups, waits):
    held, slots, _ = act_ref.shape
    cores, _, _ = back_ref.shape
    tensors, _, _, span = wds_ref.shape
    step = min(STEP, span)
    per = slots // groups
    for t in range(tensors):
        for copy in waits[t]:
            copy.wait()
        for n in range(span // step):
            cols = slice(n * step, (n + 1) * step)
            for j in range(held):
                out = jnp.dot(act_ref[j], wds_ref[t, j, :, cols], preferred_element_type=F32)
                out = out.astype(BF16)
                for g in range(groups):
                    mixed_ref[g, j * per : (j + 1) * per, :] = out[g * per : (g + 1) * per]
            for i in range(cores):
                mixed = mixed_ref[i if groups > 1 else 0]
                rows = jnp.dot(back_ref[i], mixed, preferred_element_type=F32)
                outs_ref[i * tensors + t][:, cols] = rows.astype(BF16)


def first_kernel(
    dims, place_ref, back_ref, *rest
):
    cores, tensors, depth, groups, first = dims
    lengths = depth if groups > 1 else 1
    count = cores * tensors * lengths
    pieces, rest = rest[:count], rest[count:]
    wg_ref, wu_ref, wd_ref, act_ref = rest[:4]
    outs_ref = rest[4 : 4 + cores * tensors]
    x_ref, s_ref, wgs_ref, wus_ref, wds_ref, mixed_ref, x_sem, w_sem, d_sem = rest[
        4 + cores * tensors :
    ]
    d, x = lax.axis_index("dp"), lax.axis_index("tensor")
    held = wg_ref.shape[0]
    part, cols = pieces[0].shape
    width = x_ref.shape[-1]
    copies = []
    for i in range(cores):
        at = pl.multiple_of((d + i) % cores * cols, 128)
        for k in range(tensors):
            for o in range(lengths):
                n = (i * tensors + k) * lengths + o
                g, row = (k, o) if groups > 1 else (0, k)
                copies.append(
                    pltpu.make_async_copy(
                        pieces[n],
                        x_ref.at[g, pl.ds(row * part, part), pl.ds(at, cols)],
                        x_sem.at[n],
                    )
                )
    for copy in copies:
        copy.start()
    for copy in copies:
        copy.wait()

    def weights(j):
        return [
            pltpu.make_async_copy(src.at[j], dst.at[j], w_sem.at[n, j])
            for n, (src, dst) in enumerate(((wg_ref, wgs_ref), (wu_ref, wus_ref)))
        ]

    downs = down_copies(wd_ref, wds_ref, d_sem, first)
    queue = [weights(j) for j in range(held)] + downs

    def start(n):
        if n < len(queue):
            for copy in queue[n]:
                copy.start()

    start(0)
    per = s_ref.shape[1] // groups
    step = min(STEP, width)
    for g in range(groups):
        kk = (d + g + tensors - x) % tensors if groups > 1 else 0
        for n in range(width // step):
            at = slice(n * step, (n + 1) * step)
            rows = jnp.dot(place_ref[g], x_ref[kk, :, at], preferred_element_type=F32)
            rows = rows.astype(BF16)
            for j in range(held):
                s_ref[j, g * per : (g + 1) * per, at] = rows[j * per : (j + 1) * per]
        if g == 0:
            start(1)

    for j in range(held):
        start(j + 2)
        wait_gate, wait_up = weights(j)
        wait_gate.wait()
        gate = jnp.dot(s_ref[j], wgs_ref[j], preferred_element_type=F32)
        wait_up.wait()
        up = jnp.dot(s_ref[j], wus_ref[j], preferred_element_type=F32)
        act_ref[j] = (gate / (1.0 + jnp.exp(-gate)) * up).astype(BF16)
    for n in range(held + 2, len(queue)):
        start(n)
    down_and_combine(back_ref, act_ref, wds_ref, outs_ref, mixed_ref, groups, downs)


def later_kernel(dims, back_ref, act_ref, wd_ref, *rest):
    cores, tensors, groups, first = dims
    outs_ref = rest[: cores * tensors]
    wds_ref, mixed_ref, d_sem = rest[cores * tensors :]
    downs = down_copies(wd_ref, wds_ref, d_sem, first)
    for copies in downs:
        for copy in copies:
            copy.start()
    down_and_combine(back_ref, act_ref, wds_ref, outs_ref, mixed_ref, groups, downs)


def on_device(attn, o_weight, residual, norm_gain, expert_ids, route_weights, w_gate, w_up, w_down):
    cores, tensors, depth = (lax.axis_size(a) for a in ("dp", "tensor", "expert"))
    d, x, z = (lax.axis_index(a) for a in ("dp", "tensor", "expert"))
    rows = attn.shape[0]
    width = norm_gain.shape[0]
    held, _, hidden_units = w_gate.shape
    experts = held * depth * cores
    sub = tensors // cores
    part = rows * cores // tensors
    cols_core = width // cores
    cols_out = width // tensors
    choices = expert_ids.shape[1]

    attn_all = jnp.concatenate([fetch(attn, "dp", i) for i in range(cores)], axis=0)
    res_all = jnp.concatenate([fetch(residual, "dp", i) for i in range(cores)], axis=0)
    partial = jnp.dot(attn_all, o_weight, preferred_element_type=F32)
    res_here = jnp.where(x // sub == d, res_all.astype(F32), 0.0)
    if sub == 1:
        partial = partial + res_here
    else:
        at = (x % sub) * cols_out
        partial = lax.dynamic_update_slice_in_dim(
            partial, lax.dynamic_slice_in_dim(partial, at, cols_out, 1) + res_here, at, 1
        )
    parts = partial.reshape(tensors, part, cols_core)

    def place(p):
        return ((p // sub - d) % cores) * sub + p % sub

    hidden = pick(parts, place(x))
    for k in range(1, tensors):
        sent = pick(parts, place((x - k) % tensors)).astype(BF16)
        hidden = hidden + fetch(sent, "tensor", k).astype(F32)
    hidden = hidden.astype(BF16).astype(F32)
    squares = jnp.sum(hidden * hidden, axis=1, keepdims=True)
    total = squares
    for i in range(1, cores):
        total = total + fetch(squares, "dp", i)
    inverse = lax.rsqrt(total / width + epsilon)
    gain = lax.dynamic_slice_in_dim(norm_gain, d * cols_core, cols_core, 0)
    normed = (hidden * inverse * gain.astype(F32)[None, :]).astype(BF16)

    route = pl.pallas_call(
        functools.partial(codes_kernel, experts),
        out_shape=jax.ShapeDtypeStruct((2 * choices, rows), F32),
        in_specs=[VMEM, VMEM],
        out_specs=VMEM,
        compiler_params=SMALL,
        name="codes",
    )(expert_ids, route_weights)
    route = jnp.stack([fetch(route, "dp", i) for i in range(cores)])
    routes = [route]
    for o in range(1, depth):
        routes.append(across(route, "expert", o))
    groups = tensors if sub == 1 else 1
    blocks = depth * cores // groups
    group_slots = held * blocks * SLOT
    first_code = (z * cores + d) * held * SLOT
    if groups > 1:
        placing, back = pl.pallas_call(
            functools.partial(tables_kernel, choices),
            out_shape=[
                jax.ShapeDtypeStruct((cores, group_slots, depth * rows), BF16),
                jax.ShapeDtypeStruct((cores, depth * rows, group_slots), BF16),
            ],
            in_specs=[SMEM] + [VMEM] * depth,
            out_specs=[VMEM, VMEM],
            compiler_params=SMALL,
            name="tables",
        )(first_code.astype(jnp.int32).reshape(1), *routes)
    else:
        route = jnp.stack(routes)
        local = route[:, :, :choices] - first_code.astype(F32)
        valid = (local >= 0) & (local < held * SLOT)
        which = jnp.floor(local / SLOT)
        block_ids = jnp.arange(depth, dtype=F32)[:, None, None, None]
        block_ids = block_ids * cores + jnp.arange(cores, dtype=F32)[None, :, None, None]
        slot = which * (blocks * SLOT) + block_ids * SLOT + (local - which * SLOT)
        slot = jnp.where(valid, slot, -1.0)
        weights = route[:, :, choices:]
        by_core = slot.transpose(1, 2, 0, 3).reshape(cores, choices, depth * rows, 1)
        weight_by_core = weights.transpose(1, 2, 0, 3).reshape(cores, choices, depth * rows, 1)
        slot_ids = jnp.arange(group_slots, dtype=F32)
        back = jnp.sum(jnp.where(by_core == slot_ids, weight_by_core, 0.0), axis=1).astype(BF16)
        table = slot.reshape(depth, cores, choices, sub, part)
        table = table.transpose(1, 3, 2, 0, 4).reshape(tensors, choices, depth * part)
        table = jnp.stack([pick(table, place((x + k) % tensors)) for k in range(tensors)])
        table = table.transpose(1, 0, 2).reshape(1, choices, -1)
        placing = jnp.any(table[:, :, None, :] == slot_ids[:, None], axis=1).astype(BF16)

    along = [normed]
    mine = {}
    for o in range(depth):
        if o > 0:
            along.append(across(along[o & (o - 1)], "expert", o & -o))
    if sub > 1:
        along = [jnp.concatenate(along, axis=0)]
    for o, value in enumerate(along):
        for k in range(tensors):
            mine[k, o] = fetch(value, "tensor", k)
    pieces = []
    for i in range(cores):
        for k in range(tensors):
            for o in range(len(along)):
                pieces.append(fetch(mine[k, o], "dp", i))

    slots = groups * blocks * SLOT
    spans = [cols_out * n // 8 for n in CHUNKS]
    out_rows = depth * rows

    def out_shapes(span):
        return [jax.ShapeDtypeStruct((out_rows, span), BF16)] * (cores * tensors)

    def scratch(span):
        return [
            pltpu.VMEM((tensors, held, hidden_units, span), BF16),
            pltpu.VMEM((groups, group_slots, min(STEP, span)), BF16),
        ]

    activated, *outs = pl.pallas_call(
        functools.partial(first_kernel, (cores, tensors, depth, groups, 0)),
        out_shape=[jax.ShapeDtypeStruct((held, slots, hidden_units), BF16)] + out_shapes(spans[0]),
        in_specs=[VMEM, VMEM] + [ANY] * (len(pieces) + 3),
        out_specs=[VMEM] * (1 + cores * tensors),
        scratch_shapes=[
            pltpu.VMEM((groups, tensors // groups * depth * part, width), BF16),
            pltpu.VMEM((held, slots, width), BF16),
            pltpu.VMEM(w_gate.shape, BF16),
            pltpu.VMEM(w_up.shape, BF16),
        ]
        + scratch(spans[0])
        + [
            pltpu.SemaphoreType.DMA((len(pieces),)),
            pltpu.SemaphoreType.DMA((2, held)),
            pltpu.SemaphoreType.DMA((tensors, held)),
        ],
        compiler_params=PARAMS,
        name="experts_first",
    )(placing, back, *pieces, w_gate, w_up, w_down)

    results = []
    at = 0
    for n, span in enumerate(spans):
        if n > 0:
            outs = pl.pallas_call(
                functools.partial(later_kernel, (cores, tensors, groups, at)),
                out_shape=out_shapes(span),
                in_specs=[VMEM, VMEM, ANY],
                out_specs=[VMEM] * (cores * tensors),
                scratch_shapes=scratch(span) + [pltpu.SemaphoreType.DMA((tensors, held))],
                compiler_params=PARAMS,
                cost_estimate=pl.CostEstimate(
                    flops=4 * slots * held * hidden_units * span * tensors,
                    bytes_accessed=2 * held * hidden_units * span * tensors,
                    transcendentals=0,
                ),
                name="experts_later",
            )(back, activated, w_down)
        at += span
        sides = []
        for t in list(range(1, tensors)) + [0]:
            summed = outs[t].astype(F32)
            for i in range(1, cores):
                got = fetch(outs[i * tensors + t], "dp", -i)
                summed = summed + got.astype(F32)
            if t > 0:
                got = fetch(summed.astype(BF16), "tensor", -t)
                sides.append(got)
        narrow = summed
        for got in sides:
            narrow = narrow + got.astype(F32)
        narrow = narrow.reshape(depth, rows, span)
        flip = 1
        while flip < depth:
            narrow = narrow.reshape(-1, 2, rows, span)
            got = across(narrow[:, 1].astype(BF16), "expert", flip)
            narrow = narrow[:, 0] + got.astype(F32)
            flip *= 2
        results.append(narrow[0].astype(BF16))
    return jnp.concatenate(results, axis=1)


def solution(mesh):
    placed = (
        P(("groups", "expert", "dp"), "tensor"),
        P("tensor", "dp"),
        P(("groups", "expert", "dp"), "tensor"),
        P(),
        P(("groups", "expert", "dp"), None),
        P(("groups", "expert", "dp"), None),
        P(("expert", "dp"), None, "tensor"),
        P(("expert", "dp"), None, "tensor"),
        P(("expert", "dp"), "tensor", None),
    )

    step = jax.shard_map(
        on_device,
        mesh=mesh,
        in_specs=placed,
        out_specs=P(("groups", "expert", "dp"), "tensor"),
        check_vma=False,
    )
    if mesh.shape["tensor"] != mesh.shape["dp"]:
        return step
    depth = mesh.shape["expert"]
    for _ in range(1, len(CHUNKS)):
        flip = 1
        while flip < depth:
            flip *= 2
    return step
```

```python
import functools

import jax
import jax.numpy as jnp
from jax import lax
from jax.experimental import pallas as pl
from jax.experimental.pallas import tpu as pltpu
from jax.sharding import PartitionSpec as P


SLOT = 24

epsilon = 1e-06

CHUNKS = (4, 3, 1)


def fetch(value, axis, step):
    size = lax.axis_size(axis)
    if step % size == 0:
        return value
    return lax.ppermute(value, axis, [((i + step) % size, i) for i in range(size)])


def across(value, axis, flip):
    size = lax.axis_size(axis)
    return lax.ppermute(value, axis, [(i ^ flip, i) for i in range(size)])


def pick(stacked, index):
    return lax.dynamic_index_in_dim(stacked, index, 0, keepdims=False)


STEP = 1024

F32, BF16 = jnp.float32, jnp.bfloat16
ANY = pl.BlockSpec(memory_space=pl.ANY)
VMEM = pl.BlockSpec(memory_space=pltpu.VMEM)
SMEM = pl.BlockSpec(memory_space=pltpu.SMEM)
SMALL = pltpu.CompilerParams(vmem_limit_bytes=8 * 1024 * 1024)
PARAMS = pltpu.CompilerParams(vmem_limit_bytes=60 * 1024 * 1024)


def codes_kernel(experts, ids_ref, weights_ref, out_ref):
    rows, choices = ids_ref.shape
    ids = ids_ref[...]
    lanes = lax.broadcasted_iota(jnp.int32, (rows, experts), 1)
    picked = [(ids[:, k : k + 1] == lanes).astype(F32) for k in range(choices)]
    chosen = functools.reduce(jnp.add, picked)
    earlier = lax.broadcasted_iota(jnp.int32, (rows, rows), 0) > lax.broadcasted_iota(
        jnp.int32, (rows, rows), 1
    )
    before = jnp.dot(
        earlier.astype(F32).astype(BF16), chosen.astype(BF16), preferred_element_type=F32
    )
    slot = [jnp.sum(p * before, axis=1, keepdims=True) for p in picked]
    codes = jnp.concatenate(slot, axis=1) + ids.astype(F32) * SLOT
    out_ref[...] = jnp.concatenate([codes, weights_ref[...]], axis=1).T


def tables_kernel(choices, base_ref, *rest):
    routes, (place_ref, back_ref) = rest[:-2], rest[-2:]
    depth = len(routes)
    cores, group_slots, out_rows = place_ref.shape
    per = depth * SLOT
    base = base_ref[0].astype(F32)
    for i in range(cores):
        slots = []
        for o in range(depth):
            local = routes[o][i, :choices] - base
            which = jnp.floor((local + 0.5) * (1.0 / SLOT))
            slot = which * (per - SLOT) + local + o * SLOT
            slots.append(jnp.where((local >= 0) & (local < group_slots // depth), slot, -1.0))
        slot = jnp.concatenate(slots, axis=1).astype(jnp.int32)
        down = lax.broadcasted_iota(jnp.int32, (group_slots, out_rows), 0)
        hit = [slot[k : k + 1] == down for k in range(choices)]
        place_ref[i] = functools.reduce(jnp.logical_or, hit).astype(F32).astype(BF16)
        turned = slot.astype(F32).T.astype(jnp.int32)
        weights = jnp.concatenate([routes[o][i, choices:] for o in range(depth)], axis=1).T
        along = lax.broadcasted_iota(jnp.int32, (out_rows, group_slots), 1)
        total = jnp.zeros((out_rows, group_slots), F32)
        for k in range(choices):
            total = jnp.where(turned[:, k : k + 1] == along, weights[:, k : k + 1], total)
        back_ref[i] = total.astype(BF16)


def down_copies(wd_ref, wds_ref, sem_ref, first):
    tensors, held, _, span = wds_ref.shape
    x = lax.axis_index("tensor")
    cols_out = wd_ref.shape[2] // tensors
    copies = [[] for _ in range(tensors)]
    for t in range(tensors):
        at = pl.multiple_of((x + t) % tensors * cols_out + first, 128)
        for j in range(held):
            copies[t].append(
                pltpu.make_async_copy(
                    wd_ref.at[j, :, pl.ds(at, span)], wds_ref.at[t, j], sem_ref.at[t, j]
                )
            )
    return copies


def down_and_combine(back_ref, act_ref, wds_ref, outs_ref, mixed_ref, groups, waits, spans):
    held, slots, _ = act_ref.shape
    cores, _, _ = back_ref.shape
    tensors, _, _, span = wds_ref.shape
    step = min(STEP, span)
    per = slots // groups
    for t in range(tensors):
        for copy in waits[t]:
            copy.wait()
        for n in range(span // step):
            cols = slice(n * step, (n + 1) * step)
            for j in range(held):
                out = jnp.dot(act_ref[j], wds_ref[t, j, :, cols], preferred_element_type=F32)
                out = out.astype(BF16)
                for g in range(groups):
                    mixed_ref[g, j * per : (j + 1) * per, :] = out[g * per : (g + 1) * per]
            for i in range(cores):
                mixed = mixed_ref[i if groups > 1 else 0]
                rows = jnp.dot(back_ref[i], mixed, preferred_element_type=F32)
                rows = rows.astype(BF16)
                at = 0
                for c, size in enumerate(spans):
                    low, high = max(at, n * step), min(at + size, (n + 1) * step)
                    if low < high:
                        out_ref = outs_ref[(c * cores + i) * tensors + t]
                        out_ref[:, low - at : high - at] = rows[:, low - n * step : high - n * step]
                    at += size


def first_kernel(
    dims, place_ref, back_ref, *rest
):
    cores, tensors, depth, groups, first = dims
    lengths = depth if groups > 1 else 1
    count = cores * tensors * lengths
    pieces, rest = rest[:count], rest[count:]
    wg_ref, wu_ref, wd_ref, act_ref = rest[:4]
    outs_ref = rest[4 : 4 + cores * tensors]
    x_ref, s_ref, wgs_ref, wus_ref, wds_ref, mixed_ref, x_sem, w_sem, d_sem = rest[
        4 + cores * tensors :
    ]
    d, x = lax.axis_index("dp"), lax.axis_index("tensor")
    held = wg_ref.shape[0]
    part, cols = pieces[0].shape
    width = x_ref.shape[-1]
    copies = []
    places = list(range(lengths))
    if depth == 4 and groups > 1:
        z = lax.axis_index("expert")
        inner = jnp.where((z == 1) | (z == 2), 1, 0)
        places[2:] = [2 + inner, 3 - inner]
    for i in range(cores):
        at = pl.multiple_of((d + i) % cores * cols, 128)
        for k in range(tensors):
            for o in range(lengths):
                n = (i * tensors + k) * lengths + o
                g, row = (k, places[o]) if groups > 1 else (0, k)
                row = row * part if isinstance(row, int) else pl.multiple_of(row * part, part)
                copies.append(
                    pltpu.make_async_copy(
                        pieces[n],
                        x_ref.at[g, pl.ds(row, part), pl.ds(at, cols)],
                        x_sem.at[n],
                    )
                )
    for copy in copies:
        copy.start()
    for copy in copies:
        copy.wait()

    def weights(j):
        return [
            pltpu.make_async_copy(src.at[j], dst.at[j], w_sem.at[n, j])
            for n, (src, dst) in enumerate(((wg_ref, wgs_ref), (wu_ref, wus_ref)))
        ]

    downs = down_copies(wd_ref, wds_ref, d_sem, 0)
    queue = [weights(j) for j in range(held)] + downs

    def start(n):
        if n < len(queue):
            for copy in queue[n]:
                copy.start()

    start(0)
    per = s_ref.shape[1] // groups
    step = min(STEP, width)
    for g in range(groups):
        kk = (d + g + tensors - x) % tensors if groups > 1 else 0
        for n in range(width // step):
            at = slice(n * step, (n + 1) * step)
            rows = jnp.dot(place_ref[g], x_ref[kk, :, at], preferred_element_type=F32)
            rows = rows.astype(BF16)
            for j in range(held):
                s_ref[j, g * per : (g + 1) * per, at] = rows[j * per : (j + 1) * per]
        if g == 0:
            start(1)

    for j in range(held):
        start(j + 2)
        wait_gate, wait_up = weights(j)
        wait_gate.wait()
        gate = jnp.dot(s_ref[j], wgs_ref[j], preferred_element_type=F32)
        wait_up.wait()
        up = jnp.dot(s_ref[j], wus_ref[j], preferred_element_type=F32)
        act_ref[j] = (gate / (1.0 + jnp.exp(-gate)) * up).astype(BF16)
    for n in range(held + 2, len(queue)):
        start(n)
    down_and_combine(back_ref, act_ref, wds_ref, outs_ref, mixed_ref, groups, downs, (first,))


def later_kernel(dims, back_ref, act_ref, wd_ref, *rest):
    cores, tensors, groups, first, spans = dims
    count = cores * tensors * len(spans)
    outs_ref, (wds_ref, mixed_ref, d_sem) = rest[:count], rest[count:]
    downs = down_copies(wd_ref, wds_ref, d_sem, first)
    for copies in downs:
        for copy in copies:
            copy.start()
    down_and_combine(back_ref, act_ref, wds_ref, outs_ref, mixed_ref, groups, downs, spans)


def on_device(attn, o_weight, residual, norm_gain, expert_ids, route_weights, w_gate, w_up, w_down):
    cores, tensors, depth = (lax.axis_size(a) for a in ("dp", "tensor", "expert"))
    d, x, z = (lax.axis_index(a) for a in ("dp", "tensor", "expert"))
    rows = attn.shape[0]
    width = norm_gain.shape[0]
    held, _, hidden_units = w_gate.shape
    experts = held * depth * cores
    sub = tensors // cores
    part = rows * cores // tensors
    cols_core = width // cores
    cols_out = width // tensors
    choices = expert_ids.shape[1]

    attn_all = jnp.concatenate([fetch(attn, "dp", i) for i in range(cores)], axis=0)
    res_all = jnp.concatenate([fetch(residual, "dp", i) for i in range(cores)], axis=0)
    partial = jnp.dot(attn_all, o_weight, preferred_element_type=F32)
    res_here = jnp.where(x // sub == d, res_all.astype(F32), 0.0)
    if sub == 1:
        partial = partial + res_here
    else:
        at = (x % sub) * cols_out
        partial = lax.dynamic_update_slice_in_dim(
            partial, lax.dynamic_slice_in_dim(partial, at, cols_out, 1) + res_here, at, 1
        )
    parts = partial.reshape(tensors, part, cols_core)

    def place(p):
        return ((p // sub - d) % cores) * sub + p % sub

    hidden = pick(parts, place(x))
    for k in range(1, tensors):
        sent = pick(parts, place((x - k) % tensors)).astype(BF16)
        hidden = hidden + fetch(sent, "tensor", k).astype(F32)
    hidden = hidden.astype(BF16).astype(F32)
    squares = jnp.sum(hidden * hidden, axis=1, keepdims=True)
    total = squares
    for i in range(1, cores):
        total = total + fetch(squares, "dp", i)
    inverse = lax.rsqrt(total / width + epsilon)
    gain = lax.dynamic_slice_in_dim(norm_gain, d * cols_core, cols_core, 0)
    normed = (hidden * inverse * gain.astype(F32)[None, :]).astype(BF16)

    route = pl.pallas_call(
        functools.partial(codes_kernel, experts),
        out_shape=jax.ShapeDtypeStruct((2 * choices, rows), F32),
        in_specs=[VMEM, VMEM],
        out_specs=VMEM,
        compiler_params=SMALL,
        name="codes",
    )(expert_ids, route_weights)
    route = jnp.stack([fetch(route, "dp", i) for i in range(cores)])
    routes = [route]
    for o in range(1, depth):
        routes.append(across(route, "expert", o))
    groups = tensors if sub == 1 else 1
    blocks = depth * cores // groups
    group_slots = held * blocks * SLOT
    first_code = (z * cores + d) * held * SLOT
    if groups > 1:
        placing, back = pl.pallas_call(
            functools.partial(tables_kernel, choices),
            out_shape=[
                jax.ShapeDtypeStruct((cores, group_slots, depth * rows), BF16),
                jax.ShapeDtypeStruct((cores, depth * rows, group_slots), BF16),
            ],
            in_specs=[SMEM] + [VMEM] * depth,
            out_specs=[VMEM, VMEM],
            compiler_params=SMALL,
            name="tables",
        )(first_code.astype(jnp.int32).reshape(1), *routes)
    else:
        route = jnp.stack(routes)
        local = route[:, :, :choices] - first_code.astype(F32)
        valid = (local >= 0) & (local < held * SLOT)
        which = jnp.floor(local / SLOT)
        block_ids = jnp.arange(depth, dtype=F32)[:, None, None, None]
        block_ids = block_ids * cores + jnp.arange(cores, dtype=F32)[None, :, None, None]
        slot = which * (blocks * SLOT) + block_ids * SLOT + (local - which * SLOT)
        slot = jnp.where(valid, slot, -1.0)
        weights = route[:, :, choices:]
        by_core = slot.transpose(1, 2, 0, 3).reshape(cores, choices, depth * rows, 1)
        weight_by_core = weights.transpose(1, 2, 0, 3).reshape(cores, choices, depth * rows, 1)
        slot_ids = jnp.arange(group_slots, dtype=F32)
        back = jnp.sum(jnp.where(by_core == slot_ids, weight_by_core, 0.0), axis=1).astype(BF16)
        table = slot.reshape(depth, cores, choices, sub, part)
        table = table.transpose(1, 3, 2, 0, 4).reshape(tensors, choices, depth * part)
        table = jnp.stack([pick(table, place((x + k) % tensors)) for k in range(tensors)])
        table = table.transpose(1, 0, 2).reshape(1, choices, -1)
        placing = jnp.any(table[:, :, None, :] == slot_ids[:, None], axis=1).astype(BF16)

    along = [normed]
    mine = {}
    if depth == 4 and sub == 1:
        middle, outward = ((1, 2), (2, 1)), ((1, 0), (2, 3))
        along.append(across(normed, "expert", 1))
        middle_1 = lax.ppermute(normed, "expert", middle)
        middle_2 = lax.ppermute(along[1], "expert", middle)
        outward_2 = lax.ppermute(middle_1, "expert", outward)
        outward_3 = lax.ppermute(middle_2, "expert", outward)
        outer = (z == 0) | (z == 3)
        along.append(jnp.where(outer, outward_2, middle_1))
        along.append(jnp.where(outer, outward_3, middle_2))
    else:
        for o in range(1, depth):
            along.append(across(along[o & (o - 1)], "expert", o & -o))
    if sub > 1:
        along = [jnp.concatenate(along, axis=0)]
    for o, value in enumerate(along):
        for k in range(tensors):
            mine[k, o] = fetch(value, "tensor", k)
    pieces = []
    for i in range(cores):
        for k in range(tensors):
            for o in range(len(along)):
                pieces.append(fetch(mine[k, o], "dp", i))

    slots = groups * blocks * SLOT
    spans = [cols_out * n // 8 for n in CHUNKS]
    out_rows = depth * rows

    def out_shapes(span):
        return [jax.ShapeDtypeStruct((out_rows, span), BF16)] * (cores * tensors)

    def scratch(span):
        return [
            pltpu.VMEM((tensors, held, hidden_units, span), BF16),
            pltpu.VMEM((groups, group_slots, min(STEP, span)), BF16),
        ]

    activated, *outs = pl.pallas_call(
        functools.partial(first_kernel, (cores, tensors, depth, groups, spans[0])),
        out_shape=[jax.ShapeDtypeStruct((held, slots, hidden_units), BF16)] + out_shapes(spans[0]),
        in_specs=[VMEM, VMEM] + [ANY] * (len(pieces) + 3),
        out_specs=[VMEM] * (1 + cores * tensors),
        scratch_shapes=[
            pltpu.VMEM((groups, tensors // groups * depth * part, width), BF16),
            pltpu.VMEM((held, slots, width), BF16),
            pltpu.VMEM(w_gate.shape, BF16),
            pltpu.VMEM(w_up.shape, BF16),
        ]
        + scratch(spans[0])
        + [
            pltpu.SemaphoreType.DMA((len(pieces),)),
            pltpu.SemaphoreType.DMA((2, held)),
            pltpu.SemaphoreType.DMA((tensors, held)),
        ],
        compiler_params=PARAMS,
        name="experts_first",
    )(placing, back, *pieces, w_gate, w_up, w_down)

    more = sum(spans[1:])
    outs += pl.pallas_call(
        functools.partial(later_kernel, (cores, tensors, groups, spans[0], spans[1:])),
        out_shape=[shape for span in spans[1:] for shape in out_shapes(span)],
        in_specs=[VMEM, VMEM, ANY],
        out_specs=[VMEM] * (cores * tensors * len(spans[1:])),
        scratch_shapes=scratch(more) + [pltpu.SemaphoreType.DMA((tensors, held))],
        compiler_params=PARAMS,
        cost_estimate=pl.CostEstimate(
            flops=4 * slots * held * hidden_units * more * tensors,
            bytes_accessed=2 * held * hidden_units * more * tensors,
            transcendentals=0,
        ),
        name="experts_later",
    )(back, activated, w_down)
    results = []
    for n, span in enumerate(spans):
        mixed = outs[n * cores * tensors :]
        sides = []
        for t in list(range(1, tensors)) + [0]:
            summed = mixed[t].astype(F32)
            for i in range(1, cores):
                got = fetch(mixed[i * tensors + t], "dp", -i)
                summed = summed + got.astype(F32)
            if t > 0:
                got = fetch(summed.astype(BF16), "tensor", -t)
                sides.append(got)
        narrow = summed
        for got in sides:
            narrow = narrow + got.astype(F32)
        narrow = narrow.reshape(depth, rows, span)
        flip = 1
        while flip < depth:
            narrow = narrow.reshape(-1, 2, rows, span)
            got = across(narrow[:, 1].astype(BF16), "expert", flip)
            narrow = narrow[:, 0] + got.astype(F32)
            flip *= 2
        results.append(narrow[0].astype(BF16))
    return jnp.concatenate(results, axis=1)


def solution(mesh):
    placed = (
        P(("groups", "expert", "dp"), "tensor"),
        P("tensor", "dp"),
        P(("groups", "expert", "dp"), "tensor"),
        P(),
        P(("groups", "expert", "dp"), None),
        P(("groups", "expert", "dp"), None),
        P(("expert", "dp"), None, "tensor"),
        P(("expert", "dp"), None, "tensor"),
        P(("expert", "dp"), "tensor", None),
    )

    step = jax.shard_map(
        on_device,
        mesh=mesh,
        in_specs=placed,
        out_specs=P(("groups", "expert", "dp"), "tensor"),
        check_vma=False,
    )
    if mesh.shape["tensor"] != mesh.shape["dp"]:
        return step
    depth = mesh.shape["expert"]
    for _ in range(1, len(CHUNKS)):
        flip = 1
        while flip < depth:
            flip *= 2
    return step
```

```python
import functools

import jax
import jax.numpy as jnp
from jax import lax
from jax.experimental import pallas as pl
from jax.experimental.pallas import tpu as pltpu
from jax.sharding import PartitionSpec as P


SLOT = 24

epsilon = 1e-06

CHUNKS = (4, 3, 1)


def fetch(value, axis, step):
    size = lax.axis_size(axis)
    if step % size == 0:
        return value
    return lax.ppermute(value, axis, [((i + step) % size, i) for i in range(size)])


def across(value, axis, flip):
    size = lax.axis_size(axis)
    return lax.ppermute(value, axis, [(i ^ flip, i) for i in range(size)])


def pick(stacked, index):
    return lax.dynamic_index_in_dim(stacked, index, 0, keepdims=False)


STEP = 1024

F32, BF16 = jnp.float32, jnp.bfloat16
VMEM = pl.BlockSpec(memory_space=pltpu.VMEM)
HBM = pl.BlockSpec(memory_space=pltpu.HBM)
SMALL = pltpu.CompilerParams(vmem_limit_bytes=8 * 1024 * 1024)
PARAMS = pltpu.CompilerParams(vmem_limit_bytes=60 * 1024 * 1024)


def codes_kernel(experts, count, ids_ref, weights_ref, *rest):
    far, out_ref, near, sem_ref = rest[:count], rest[count], rest[count + 1 : -1], rest[-1]
    copies = [
        pltpu.make_async_copy(src, dst, sem_ref.at[n]) for n, (src, dst) in enumerate(zip(far, near))
    ]
    for copy in copies:
        copy.start()
    choices, rows = ids_ref.shape
    ids = ids_ref[...].astype(F32).T.astype(jnp.int32)
    lanes = lax.broadcasted_iota(jnp.int32, (rows, experts), 1)
    picked = [(ids[:, k : k + 1] == lanes).astype(F32) for k in range(choices)]
    chosen = functools.reduce(jnp.add, picked)
    earlier = lax.broadcasted_iota(jnp.int32, (rows, rows), 0) > lax.broadcasted_iota(
        jnp.int32, (rows, rows), 1
    )
    before = jnp.dot(
        earlier.astype(F32).astype(BF16), chosen.astype(BF16), preferred_element_type=F32
    )
    slot = [jnp.sum(p * before, axis=1, keepdims=True) for p in picked]
    codes = jnp.concatenate(slot, axis=1) + ids.astype(F32) * SLOT
    out_ref[:choices] = codes.T
    out_ref[choices:] = weights_ref[...]
    for copy in copies:
        copy.wait()


def tables_kernel(choices, *rest):
    routes, (place_ref, back_ref) = rest[:-2], rest[-2:]
    depth = len(routes)
    cores, group_slots, out_rows = place_ref.shape
    per = depth * SLOT
    z = lax.axis_index("expert")
    index = z * cores + lax.axis_index("dp")
    base = (index * (group_slots // depth)).astype(F32)
    for i in range(cores):
        slots = []
        for o in range(depth):
            local = routes[o][i, :choices] - base
            which = jnp.floor((local + 0.5) * (1.0 / SLOT))
            slot = which * (per - SLOT) + local + o * SLOT
            slots.append(jnp.where((local >= 0) & (local < group_slots // depth), slot, -1.0))
        slot = jnp.concatenate(slots, axis=1).astype(jnp.int32)
        down = lax.broadcasted_iota(jnp.int32, (group_slots, out_rows), 0)
        if depth == 4:
            inner = (z > 0) & (z < depth - 1)
            second, third = jnp.where(inner, slots[3], slots[2]), jnp.where(inner, slots[2], slots[3])
            arrived = jnp.concatenate(slots[:2] + [second, third], axis=1).astype(jnp.int32)
        else:
            arrived = slot
        hit = [arrived[k : k + 1] == down for k in range(choices)]
        place_ref[i] = functools.reduce(jnp.logical_or, hit).astype(F32).astype(BF16)
        turned = slot.astype(F32).T.astype(jnp.int32)
        weights = jnp.concatenate([routes[o][i, choices:] for o in range(depth)], axis=1).T
        along = lax.broadcasted_iota(jnp.int32, (out_rows, group_slots), 1)
        total = jnp.zeros((out_rows, group_slots), F32)
        for k in range(choices):
            total = jnp.where(turned[:, k : k + 1] == along, weights[:, k : k + 1], total)
        back_ref[i] = total.astype(BF16)


def project_kernel(attn_ref, attn_got_ref, res_ref, res_got_ref, weight_ref, kept_ref, sent_ref):
    same = lax.axis_index("tensor") == lax.axis_index("dp")
    weight = weight_ref[...]
    own = jnp.dot(attn_ref[...], weight, preferred_element_type=F32)
    other = jnp.dot(attn_got_ref[...], weight, preferred_element_type=F32)
    own_sum = own + res_ref[...].astype(F32)
    other_sum = other + res_got_ref[...].astype(F32)
    kept_ref[...] = jnp.where(same, own_sum, other)
    sent_ref[...] = jnp.where(same, other_sum, own).astype(BF16)


def down_copies(wd_ref, wds_ref, sem_ref, first):
    tensors, held, _, span = wds_ref.shape
    x = lax.axis_index("tensor")
    cols_out = wd_ref.shape[2] // tensors
    copies = [[] for _ in range(tensors)]
    for t in range(tensors):
        at = pl.multiple_of((x + t) % tensors * cols_out + first, 128)
        for j in range(held):
            copies[t].append(
                pltpu.make_async_copy(
                    wd_ref.at[j, :, pl.ds(at, span)], wds_ref.at[t, j], sem_ref.at[t, j]
                )
            )
    return copies


def down_and_combine(back_ref, act_ref, wds_ref, outs_ref, mixed_ref, groups, waits, spans):
    held, slots, _ = act_ref.shape
    cores, _, _ = back_ref.shape
    tensors, _, _, span = wds_ref.shape
    step = min(STEP, span)
    per = slots // groups
    for t in range(tensors):
        for copy in waits[t]:
            copy.wait()
        for n in range(span // step):
            cols = slice(n * step, (n + 1) * step)
            for j in range(held):
                out = jnp.dot(act_ref[j], wds_ref[t, j, :, cols], preferred_element_type=F32)
                out = out.astype(BF16)
                for g in range(groups):
                    mixed_ref[g, j * per : (j + 1) * per, :] = out[g * per : (g + 1) * per]
            for i in range(cores):
                mixed = mixed_ref[i if groups > 1 else 0]
                rows = jnp.dot(back_ref[i], mixed, preferred_element_type=F32)
                rows = rows.astype(BF16)
                at = 0
                for c, size in enumerate(spans):
                    low, high = max(at, n * step), min(at + size, (n + 1) * step)
                    if low < high:
                        out_ref = outs_ref[(c * cores + i) * tensors + t]
                        out_ref[:, low - at : high - at] = rows[:, low - n * step : high - n * step]
                    at += size


def first_kernel(dims, place_ref, back_ref, *rest):
    cores, tensors, lengths, groups, first = dims
    count = cores * tensors * lengths
    pieces, rest = rest[:count], rest[count:]
    wg_ref, wu_ref, wd_ref, act_ref = rest[:4]
    outs_ref = rest[4 : 4 + cores * tensors]
    s_ref, wgs_ref, wus_ref, wds_ref, mixed_ref, w_sem, d_sem = rest[4 + cores * tensors :]
    d, x = lax.axis_index("dp"), lax.axis_index("tensor")
    held, slots, _ = s_ref.shape
    cols = pieces[0].shape[1]

    def weights(j):
        return [
            pltpu.make_async_copy(src.at[j], dst.at[j], w_sem.at[n, j])
            for n, (src, dst) in enumerate(((wg_ref, wgs_ref), (wu_ref, wus_ref)))
        ]

    downs = down_copies(wd_ref, wds_ref, d_sem, 0)
    queue = [weights(j) for j in range(held)] + downs

    def start(n):
        if n < len(queue):
            for copy in queue[n]:
                copy.start()

    start(0)
    per = slots // groups
    step = min(STEP, cols)
    for k in range(groups):
        g = (x + k + cores - d) % cores if groups > 1 else 0
        place = place_ref[g]
        at_rows = pl.ds(pl.multiple_of(g * per, per), per) if groups > 1 else slice(0, per)
        for i in range(cores):
            base = (d + i) % cores * cols
            first_piece = (i * tensors + k) * lengths
            blocks = pieces[first_piece : first_piece + count // (cores * groups)]
            for n in range(cols // step):
                take = slice(n * step, (n + 1) * step)
                rows = jnp.concatenate([block[:, take] for block in blocks], axis=0)
                rows = jnp.dot(place, rows, preferred_element_type=F32).astype(BF16)
                at = pl.ds(pl.multiple_of(base + n * step, step), step)
                for j in range(held):
                    s_ref[j, at_rows, at] = rows[j * per : (j + 1) * per]

        if k == 0:
            start(1)

    for j in range(held):
        start(j + 2)
        wait_gate, wait_up = weights(j)
        wait_gate.wait()
        gate = jnp.dot(s_ref[j], wgs_ref[j], preferred_element_type=F32)
        wait_up.wait()
        up = jnp.dot(s_ref[j], wus_ref[j], preferred_element_type=F32)
        act_ref[j] = (gate / (1.0 + jnp.exp(-gate)) * up).astype(BF16)
    for n in range(held + 2, len(queue)):
        start(n)
    down_and_combine(back_ref, act_ref, wds_ref, outs_ref, mixed_ref, groups, downs, (first,))


def later_kernel(dims, back_ref, act_ref, wd_ref, *rest):
    cores, tensors, groups, first, spans = dims
    count = cores * tensors * len(spans)
    outs_ref, (wds_ref, mixed_ref, d_sem) = rest[:count], rest[count:]
    downs = down_copies(wd_ref, wds_ref, d_sem, first)
    for copies in downs:
        for copy in copies:
            copy.start()
    down_and_combine(back_ref, act_ref, wds_ref, outs_ref, mixed_ref, groups, downs, spans)


def on_device(attn, o_weight, residual, norm_gain, expert_ids, route_weights, w_gate, w_up, w_down):
    cores, tensors, depth = (lax.axis_size(a) for a in ("dp", "tensor", "expert"))
    d, x, z = (lax.axis_index(a) for a in ("dp", "tensor", "expert"))
    rows = attn.shape[0]
    width = norm_gain.shape[0]
    held, _, hidden_units = w_gate.shape
    experts = held * depth * cores
    sub = tensors // cores
    part = rows * cores // tensors
    cols_core = width // cores
    cols_out = width // tensors
    choices = expert_ids.shape[1]

    far = [o_weight, attn, residual] if cores == 2 and sub == 1 else []
    route, *near = pl.pallas_call(
        functools.partial(codes_kernel, experts, len(far)),
        out_shape=[jax.ShapeDtypeStruct((2 * choices, rows), F32)]
        + [pltpu.VMEM(v.shape, v.dtype) for v in far],
        in_specs=[VMEM, VMEM] + [HBM] * len(far),
        out_specs=[VMEM] * (1 + len(far)),
        scratch_shapes=[pltpu.SemaphoreType.DMA((len(far) + 1,))],
        compiler_params=pltpu.CompilerParams(vmem_limit_bytes=50 * 1024 * 1024),
        name="codes",
    )(expert_ids.T, route_weights.T, *far)

    def place(p):
        return ((p // sub - d) % cores) * sub + p % sub

    if cores == 2 and sub == 1:
        attn_got = fetch(attn, "dp", 1)
        res_got = fetch(residual, "dp", 1)
        hidden, sent = pl.pallas_call(
            project_kernel,
            out_shape=[
                jax.ShapeDtypeStruct((part, cols_core), F32),
                jax.ShapeDtypeStruct((part, cols_core), BF16),
            ],
            in_specs=[VMEM] * 5,
            out_specs=[VMEM] * 2,
            compiler_params=pltpu.CompilerParams(vmem_limit_bytes=24 * 1024 * 1024),
            name="project",
        )(near[1], attn_got, near[2], res_got, near[0])
        hidden = hidden + fetch(sent, "tensor", 1).astype(F32)
    else:
        attn_all = jnp.concatenate([fetch(attn, "dp", i) for i in range(cores)], axis=0)
        res_all = jnp.concatenate([fetch(residual, "dp", i) for i in range(cores)], axis=0)
        partial = jnp.dot(attn_all, o_weight, preferred_element_type=F32)
        res_here = jnp.where(x // sub == d, res_all.astype(F32), 0.0)
        if sub == 1:
            partial = partial + res_here
        else:
            at = (x % sub) * cols_out
            partial = lax.dynamic_update_slice_in_dim(
                partial, lax.dynamic_slice_in_dim(partial, at, cols_out, 1) + res_here, at, 1
            )
        parts = partial.reshape(tensors, part, cols_core)

        hidden = pick(parts, place(x))
        for k in range(1, tensors):
            sent = pick(parts, place((x - k) % tensors)).astype(BF16)
            hidden = hidden + fetch(sent, "tensor", k).astype(F32)
    hidden = hidden.astype(BF16).astype(F32)
    squares = jnp.sum(hidden * hidden, axis=1, keepdims=True)
    total = squares
    for i in range(1, cores):
        total = total + fetch(squares, "dp", i)
    inverse = lax.rsqrt(total / width + epsilon)
    gain = lax.dynamic_slice_in_dim(norm_gain, d * cols_core, cols_core, 0)
    normed = (hidden * inverse * gain.astype(F32)[None, :]).astype(BF16)

    route = jnp.stack([fetch(route, "dp", i) for i in range(cores)])
    routes = [route]
    for o in range(1, depth):
        routes.append(across(route, "expert", o))
    groups = tensors if sub == 1 else 1
    blocks = depth * cores // groups
    group_slots = held * blocks * SLOT
    first_code = (z * cores + d) * held * SLOT
    if groups > 1:
        placing, back = pl.pallas_call(
            functools.partial(tables_kernel, choices),
            out_shape=[
                jax.ShapeDtypeStruct((cores, group_slots, depth * rows), BF16),
                jax.ShapeDtypeStruct((cores, depth * rows, group_slots), BF16),
            ],
            in_specs=[VMEM] * depth,
            out_specs=[VMEM, VMEM],
            compiler_params=SMALL,
            name="tables",
        )(*routes)
    else:
        route = jnp.stack(routes)
        local = route[:, :, :choices] - first_code.astype(F32)
        valid = (local >= 0) & (local < held * SLOT)
        which = jnp.floor(local / SLOT)
        block_ids = jnp.arange(depth, dtype=F32)[:, None, None, None]
        block_ids = block_ids * cores + jnp.arange(cores, dtype=F32)[None, :, None, None]
        slot = which * (blocks * SLOT) + block_ids * SLOT + (local - which * SLOT)
        slot = jnp.where(valid, slot, -1.0)
        weights = route[:, :, choices:]
        by_core = slot.transpose(1, 2, 0, 3).reshape(cores, choices, depth * rows, 1)
        weight_by_core = weights.transpose(1, 2, 0, 3).reshape(cores, choices, depth * rows, 1)
        slot_ids = jnp.arange(group_slots, dtype=F32)
        back = jnp.sum(jnp.where(by_core == slot_ids, weight_by_core, 0.0), axis=1).astype(BF16)
        table = slot.reshape(depth, cores, choices, sub, part)
        table = table.transpose(1, 3, 2, 0, 4).reshape(tensors, choices, depth * part)
        table = jnp.stack([pick(table, place((x + k) % tensors)) for k in range(tensors)])
        table = table.transpose(1, 0, 2).reshape(1, choices, -1)
        placing = jnp.any(table[:, :, None, :] == slot_ids[:, None], axis=1).astype(BF16)

    along = [normed]
    mine = {}
    if depth == 4 and sub == 1:
        middle, outward = ((1, 2), (2, 1)), ((1, 0), (2, 3))
        along.append(across(normed, "expert", 1))
        middle_1 = lax.ppermute(normed, "expert", middle)
        middle_2 = lax.ppermute(along[1], "expert", middle)
        outward_2 = lax.ppermute(middle_1, "expert", outward)
        outward_3 = lax.ppermute(middle_2, "expert", outward)
        outer = (z == 0) | (z == 3)
        along.append(jnp.where(outer, outward_2, middle_1))
        along.append(jnp.where(outer, outward_3, middle_2))
    else:
        for o in range(1, depth):
            along.append(across(along[o & (o - 1)], "expert", o & -o))
    if sub > 1:
        along = [jnp.concatenate(along, axis=0)]
    for o, value in enumerate(along):
        for k in range(tensors):
            mine[k, o] = fetch(value, "tensor", k)
    pieces = []
    for i in range(cores):
        for k in range(tensors):
            for o in range(len(along)):
                pieces.append(fetch(mine[k, o], "dp", i))

    slots = groups * blocks * SLOT
    spans = [cols_out * n // 8 for n in CHUNKS]
    out_rows = depth * rows

    def out_shapes(span):
        return [jax.ShapeDtypeStruct((out_rows, span), BF16)] * (cores * tensors)

    def scratch(span):
        return [
            pltpu.VMEM((tensors, held, hidden_units, span), BF16),
            pltpu.VMEM((groups, group_slots, min(STEP, span)), BF16),
        ]

    lengths = depth if groups > 1 else 1
    activated, *outs = pl.pallas_call(
        functools.partial(first_kernel, (cores, tensors, lengths, groups, spans[0])),
        out_shape=[jax.ShapeDtypeStruct((held, slots, hidden_units), BF16)] + out_shapes(spans[0]),
        in_specs=[VMEM] * (2 + len(pieces)) + [HBM] * 3,
        out_specs=[VMEM] * (1 + cores * tensors),
        scratch_shapes=[
            pltpu.VMEM((held, slots, width), BF16),
            pltpu.VMEM(w_gate.shape, BF16),
            pltpu.VMEM(w_up.shape, BF16),
        ]
        + scratch(spans[0])
        + [pltpu.SemaphoreType.DMA((2, held)), pltpu.SemaphoreType.DMA((tensors, held))],
        compiler_params=pltpu.CompilerParams(vmem_limit_bytes=56 * 1024 * 1024),
        name="experts_first",
    )(placing, back, *pieces, w_gate, w_up, w_down)

    more = sum(spans[1:])
    outs += pl.pallas_call(
        functools.partial(later_kernel, (cores, tensors, groups, spans[0], spans[1:])),
        out_shape=[shape for span in spans[1:] for shape in out_shapes(span)],
        in_specs=[VMEM, VMEM, HBM],
        out_specs=[VMEM] * (cores * tensors * len(spans[1:])),
        scratch_shapes=scratch(more) + [pltpu.SemaphoreType.DMA((tensors, held))],
        compiler_params=PARAMS,
        cost_estimate=pl.CostEstimate(
            flops=4 * slots * held * hidden_units * more * tensors,
            bytes_accessed=2 * held * hidden_units * more * tensors,
            transcendentals=0,
        ),
        name="experts_later",
    )(back, activated, w_down)
    results = []
    for n, span in enumerate(spans):
        mixed = outs[n * cores * tensors :]
        sides = []
        for t in list(range(1, tensors)) + [0]:
            summed = mixed[t].astype(F32)
            for i in range(1, cores):
                got = fetch(mixed[i * tensors + t], "dp", -i)
                summed = summed + got.astype(F32)
            if t > 0:
                got = fetch(summed.astype(BF16), "tensor", -t)
                sides.append(got)
        narrow = summed
        for got in sides:
            narrow = narrow + got.astype(F32)
        narrow = narrow.reshape(depth, rows, span)
        flip = 1
        if depth == 4 and n + 1 == len(spans):
            whole = narrow[0]
            for o in range(1, depth):
                got = across(narrow[o].astype(BF16), "expert", o)
                whole = whole + got.astype(F32)
            results.append(whole.astype(BF16))
            continue
        while flip < depth:
            narrow = narrow.reshape(-1, 2, rows, span)
            got = across(narrow[:, 1].astype(BF16), "expert", flip)
            narrow = narrow[:, 0] + got.astype(F32)
            flip *= 2
        results.append(narrow[0].astype(BF16))
    return jnp.concatenate(results, axis=1)


def solution(mesh):
    placed = (
        P(("groups", "expert", "dp"), "tensor"),
        P("tensor", "dp"),
        P(("groups", "expert", "dp"), "tensor"),
        P(),
        P(("groups", "expert", "dp"), None),
        P(("groups", "expert", "dp"), None),
        P(("expert", "dp"), None, "tensor"),
        P(("expert", "dp"), None, "tensor"),
        P(("expert", "dp"), "tensor", None),
    )

    step = jax.shard_map(
        on_device,
        mesh=mesh,
        in_specs=placed,
        out_specs=P(("groups", "expert", "dp"), "tensor"),
        check_vma=False,
    )
    if mesh.shape["tensor"] != mesh.shape["dp"]:
        return step
    return step
```

```python
import functools

import jax
import jax.numpy as jnp
from jax import lax
from jax.experimental import pallas as pl
from jax.experimental.pallas import tpu as pltpu
from jax.sharding import PartitionSpec as P


SLOT = 24

epsilon = 1e-06

CHUNKS = (4, 3, 1)


def fetch(value, axis, step):
    size = lax.axis_size(axis)
    if step % size == 0:
        return value
    return lax.ppermute(value, axis, [((i + step) % size, i) for i in range(size)])


def across(value, axis, flip):
    size = lax.axis_size(axis)
    return lax.ppermute(value, axis, [(i ^ flip, i) for i in range(size)])


def pick(stacked, index):
    return lax.dynamic_index_in_dim(stacked, index, 0, keepdims=False)


STEP = 1024

F32, BF16 = jnp.float32, jnp.bfloat16
VMEM = pl.BlockSpec(memory_space=pltpu.VMEM)
HBM = pl.BlockSpec(memory_space=pltpu.HBM)
SMALL = pltpu.CompilerParams(vmem_limit_bytes=8 * 1024 * 1024)
PARAMS = pltpu.CompilerParams(vmem_limit_bytes=60 * 1024 * 1024)


def codes_kernel(experts, ids_ref, weights_ref, out_ref):
    choices, rows = ids_ref.shape
    ids = ids_ref[...].astype(F32).T.astype(jnp.int32)
    lanes = lax.broadcasted_iota(jnp.int32, (rows, experts), 1)
    picked = [(ids[:, k : k + 1] == lanes).astype(F32) for k in range(choices)]
    chosen = functools.reduce(jnp.add, picked)
    earlier = lax.broadcasted_iota(jnp.int32, (rows, rows), 0) > lax.broadcasted_iota(
        jnp.int32, (rows, rows), 1
    )
    before = jnp.dot(
        earlier.astype(F32).astype(BF16), chosen.astype(BF16), preferred_element_type=F32
    )
    slot = [jnp.sum(p * before, axis=1, keepdims=True) for p in picked]
    codes = jnp.concatenate(slot, axis=1) + ids.astype(F32) * SLOT
    out_ref[:choices] = codes.T
    out_ref[choices:] = weights_ref[...]


def tables_kernel(choices, *rest):
    routes, (place_ref, back_ref) = rest[:-2], rest[-2:]
    depth = len(routes)
    cores, group_slots, out_rows = place_ref.shape
    per = depth * SLOT
    z = lax.axis_index("expert")
    index = z * cores + lax.axis_index("dp")
    base = (index * (group_slots // depth)).astype(F32)
    for i in range(cores):
        slots = []
        for o in range(depth):
            local = routes[o][i, :choices] - base
            which = jnp.floor((local + 0.5) * (1.0 / SLOT))
            slot = which * (per - SLOT) + local + o * SLOT
            slots.append(jnp.where((local >= 0) & (local < group_slots // depth), slot, -1.0))
        slot = jnp.concatenate(slots, axis=1).astype(jnp.int32)
        down = lax.broadcasted_iota(jnp.int32, (group_slots, out_rows), 0)
        if depth == 4:
            inner = (z > 0) & (z < depth - 1)
            second, third = jnp.where(inner, slots[3], slots[2]), jnp.where(inner, slots[2], slots[3])
            arrived = jnp.concatenate(slots[:2] + [second, third], axis=1).astype(jnp.int32)
        else:
            arrived = slot
        hit = [arrived[k : k + 1] == down for k in range(choices)]
        place_ref[i] = functools.reduce(jnp.logical_or, hit).astype(F32).astype(BF16)
        turned = slot.astype(F32).T.astype(jnp.int32)
        weights = jnp.concatenate([routes[o][i, choices:] for o in range(depth)], axis=1).T
        along = lax.broadcasted_iota(jnp.int32, (out_rows, group_slots), 1)
        total = jnp.zeros((out_rows, group_slots), F32)
        for k in range(choices):
            total = jnp.where(turned[:, k : k + 1] == along, weights[:, k : k + 1], total)
        back_ref[i] = total.astype(BF16)


def down_copies(wd_ref, wds_ref, sem_ref, first):
    tensors, held, _, span = wds_ref.shape
    x = lax.axis_index("tensor")
    cols_out = wd_ref.shape[2] // tensors
    copies = [[] for _ in range(tensors)]
    for t in range(tensors):
        at = pl.multiple_of((x + t) % tensors * cols_out + first, 128)
        for j in range(held):
            copies[t].append(
                pltpu.make_async_copy(
                    wd_ref.at[j, :, pl.ds(at, span)], wds_ref.at[t, j], sem_ref.at[t, j]
                )
            )
    return copies


def down_and_combine(back_ref, act_ref, wds_ref, outs_ref, mixed_ref, groups, waits, spans):
    held, slots, _ = act_ref.shape
    cores, _, _ = back_ref.shape
    tensors, _, _, span = wds_ref.shape
    step = min(STEP, span)
    per = slots // groups
    for t in range(tensors):
        for copy in waits[t]:
            copy.wait()
        for n in range(span // step):
            cols = slice(n * step, (n + 1) * step)
            for j in range(held):
                out = jnp.dot(act_ref[j], wds_ref[t, j, :, cols], preferred_element_type=F32)
                out = out.astype(BF16)
                for g in range(groups):
                    mixed_ref[g, j * per : (j + 1) * per, :] = out[g * per : (g + 1) * per]
            for i in range(cores):
                mixed = mixed_ref[i if groups > 1 else 0]
                rows = jnp.dot(back_ref[i], mixed, preferred_element_type=F32)
                rows = rows.astype(BF16)
                at = 0
                for c, size in enumerate(spans):
                    low, high = max(at, n * step), min(at + size, (n + 1) * step)
                    if low < high:
                        out_ref = outs_ref[(c * cores + i) * tensors + t]
                        out_ref[:, low - at : high - at] = rows[:, low - n * step : high - n * step]
                    at += size


def first_kernel(dims, place_ref, back_ref, *rest):
    cores, tensors, lengths, groups, first = dims
    count = cores * tensors * lengths
    pieces, rest = rest[:count], rest[count:]
    wg_ref, wu_ref, wd_ref, act_ref = rest[:4]
    outs_ref = rest[4 : 4 + cores * tensors]
    s_ref, wgs_ref, wus_ref, wds_ref, mixed_ref, w_sem, d_sem = rest[4 + cores * tensors :]
    d, x = lax.axis_index("dp"), lax.axis_index("tensor")
    held, slots, _ = s_ref.shape
    cols = pieces[0].shape[1]

    def weights(j):
        return [
            pltpu.make_async_copy(src.at[j], dst.at[j], w_sem.at[n, j])
            for n, (src, dst) in enumerate(((wg_ref, wgs_ref), (wu_ref, wus_ref)))
        ]

    downs = down_copies(wd_ref, wds_ref, d_sem, 0)
    queue = [weights(j) for j in range(held)] + downs

    def start(n):
        if n < len(queue):
            for copy in queue[n]:
                copy.start()

    start(0)
    per = slots // groups
    step = min(STEP, cols)
    for k in range(groups):
        g = (x + k + cores - d) % cores if groups > 1 else 0
        place = place_ref[g]
        at_rows = pl.ds(pl.multiple_of(g * per, per), per) if groups > 1 else slice(0, per)
        for i in range(cores):
            base = (d + i) % cores * cols
            first_piece = (i * tensors + k) * lengths
            blocks = pieces[first_piece : first_piece + count // (cores * groups)]
            for n in range(cols // step):
                take = slice(n * step, (n + 1) * step)
                rows = jnp.concatenate([block[:, take] for block in blocks], axis=0)
                rows = jnp.dot(place, rows, preferred_element_type=F32).astype(BF16)
                at = pl.ds(pl.multiple_of(base + n * step, step), step)
                for j in range(held):
                    s_ref[j, at_rows, at] = rows[j * per : (j + 1) * per]

        if k == 0:
            start(1)

    for j in range(held):
        start(j + 2)
        wait_gate, wait_up = weights(j)
        wait_gate.wait()
        gate = jnp.dot(s_ref[j], wgs_ref[j], preferred_element_type=F32)
        wait_up.wait()
        up = jnp.dot(s_ref[j], wus_ref[j], preferred_element_type=F32)
        act_ref[j] = (gate / (1.0 + jnp.exp(-gate)) * up).astype(BF16)
    for n in range(held + 2, len(queue)):
        start(n)
    down_and_combine(back_ref, act_ref, wds_ref, outs_ref, mixed_ref, groups, downs, (first,))


def later_kernel(dims, back_ref, act_ref, wd_ref, *rest):
    cores, tensors, groups, first, spans = dims
    count = cores * tensors * len(spans)
    outs_ref, (wds_ref, mixed_ref, d_sem) = rest[:count], rest[count:]
    downs = down_copies(wd_ref, wds_ref, d_sem, first)
    for copies in downs:
        for copy in copies:
            copy.start()
    down_and_combine(back_ref, act_ref, wds_ref, outs_ref, mixed_ref, groups, downs, spans)


def on_device(attn, o_weight, residual, norm_gain, expert_ids, route_weights, w_gate, w_up, w_down):
    cores, tensors, depth = (lax.axis_size(a) for a in ("dp", "tensor", "expert"))
    d, x, z = (lax.axis_index(a) for a in ("dp", "tensor", "expert"))
    rows = attn.shape[0]
    width = norm_gain.shape[0]
    held, _, hidden_units = w_gate.shape
    experts = held * depth * cores
    sub = tensors // cores
    part = rows * cores // tensors
    cols_core = width // cores
    cols_out = width // tensors
    choices = expert_ids.shape[1]

    attn_all = jnp.concatenate([fetch(attn, "dp", i) for i in range(cores)], axis=0)
    res_all = jnp.concatenate([fetch(residual, "dp", i) for i in range(cores)], axis=0)
    partial = jnp.dot(attn_all, o_weight, preferred_element_type=F32)
    res_here = jnp.where(x // sub == d, res_all.astype(F32), 0.0)
    if sub == 1:
        partial = partial + res_here
    else:
        at = (x % sub) * cols_out
        partial = lax.dynamic_update_slice_in_dim(
            partial, lax.dynamic_slice_in_dim(partial, at, cols_out, 1) + res_here, at, 1
        )
    parts = partial.reshape(tensors, part, cols_core)

    def place(p):
        return ((p // sub - d) % cores) * sub + p % sub

    hidden = pick(parts, place(x))
    for k in range(1, tensors):
        sent = pick(parts, place((x - k) % tensors)).astype(BF16)
        hidden = hidden + fetch(sent, "tensor", k).astype(F32)
    hidden = hidden.astype(BF16).astype(F32)
    squares = jnp.sum(hidden * hidden, axis=1, keepdims=True)
    total = squares
    for i in range(1, cores):
        total = total + fetch(squares, "dp", i)
    inverse = lax.rsqrt(total / width + epsilon)
    gain = lax.dynamic_slice_in_dim(norm_gain, d * cols_core, cols_core, 0)
    normed = (hidden * inverse * gain.astype(F32)[None, :]).astype(BF16)

    route = pl.pallas_call(
        functools.partial(codes_kernel, experts),
        out_shape=jax.ShapeDtypeStruct((2 * choices, rows), F32),
        in_specs=[VMEM, VMEM],
        out_specs=VMEM,
        compiler_params=SMALL,
        name="codes",
    )(expert_ids.T, route_weights.T)
    route = jnp.stack([fetch(route, "dp", i) for i in range(cores)])
    routes = [route]
    for o in range(1, depth):
        routes.append(across(route, "expert", o))
    groups = tensors if sub == 1 else 1
    blocks = depth * cores // groups
    group_slots = held * blocks * SLOT
    first_code = (z * cores + d) * held * SLOT
    if groups > 1:
        placing, back = pl.pallas_call(
            functools.partial(tables_kernel, choices),
            out_shape=[
                jax.ShapeDtypeStruct((cores, group_slots, depth * rows), BF16),
                jax.ShapeDtypeStruct((cores, depth * rows, group_slots), BF16),
            ],
            in_specs=[VMEM] * depth,
            out_specs=[VMEM, VMEM],
            compiler_params=SMALL,
            name="tables",
        )(*routes)
    else:
        route = jnp.stack(routes)
        local = route[:, :, :choices] - first_code.astype(F32)
        valid = (local >= 0) & (local < held * SLOT)
        which = jnp.floor(local / SLOT)
        block_ids = jnp.arange(depth, dtype=F32)[:, None, None, None]
        block_ids = block_ids * cores + jnp.arange(cores, dtype=F32)[None, :, None, None]
        slot = which * (blocks * SLOT) + block_ids * SLOT + (local - which * SLOT)
        slot = jnp.where(valid, slot, -1.0)
        weights = route[:, :, choices:]
        by_core = slot.transpose(1, 2, 0, 3).reshape(cores, choices, depth * rows, 1)
        weight_by_core = weights.transpose(1, 2, 0, 3).reshape(cores, choices, depth * rows, 1)
        slot_ids = jnp.arange(group_slots, dtype=F32)
        back = jnp.sum(jnp.where(by_core == slot_ids, weight_by_core, 0.0), axis=1).astype(BF16)
        table = slot.reshape(depth, cores, choices, sub, part)
        table = table.transpose(1, 3, 2, 0, 4).reshape(tensors, choices, depth * part)
        table = jnp.stack([pick(table, place((x + k) % tensors)) for k in range(tensors)])
        table = table.transpose(1, 0, 2).reshape(1, choices, -1)
        placing = jnp.any(table[:, :, None, :] == slot_ids[:, None], axis=1).astype(BF16)

    along = [normed]
    mine = {}
    if depth == 4 and sub == 1:
        middle, outward = ((1, 2), (2, 1)), ((1, 0), (2, 3))
        along.append(across(normed, "expert", 1))
        middle_1 = lax.ppermute(normed, "expert", middle)
        middle_2 = lax.ppermute(along[1], "expert", middle)
        outward_2 = lax.ppermute(middle_1, "expert", outward)
        outward_3 = lax.ppermute(middle_2, "expert", outward)
        outer = (z == 0) | (z == 3)
        along.append(jnp.where(outer, outward_2, middle_1))
        along.append(jnp.where(outer, outward_3, middle_2))
    else:
        for o in range(1, depth):
            along.append(across(along[o & (o - 1)], "expert", o & -o))
    if sub > 1:
        along = [jnp.concatenate(along, axis=0)]
    for o, value in enumerate(along):
        for k in range(tensors):
            mine[k, o] = fetch(value, "tensor", k)
    pieces = []
    for i in range(cores):
        for k in range(tensors):
            for o in range(len(along)):
                pieces.append(fetch(mine[k, o], "dp", i))

    slots = groups * blocks * SLOT
    spans = [cols_out * n // 8 for n in CHUNKS]
    out_rows = depth * rows

    def out_shapes(span):
        return [jax.ShapeDtypeStruct((out_rows, span), BF16)] * (cores * tensors)

    def scratch(span):
        return [
            pltpu.VMEM((tensors, held, hidden_units, span), BF16),
            pltpu.VMEM((groups, group_slots, min(STEP, span)), BF16),
        ]

    lengths = depth if groups > 1 else 1
    activated, *outs = pl.pallas_call(
        functools.partial(first_kernel, (cores, tensors, lengths, groups, spans[0])),
        out_shape=[jax.ShapeDtypeStruct((held, slots, hidden_units), BF16)] + out_shapes(spans[0]),
        in_specs=[VMEM] * (2 + len(pieces)) + [HBM] * 3,
        out_specs=[VMEM] * (1 + cores * tensors),
        scratch_shapes=[
            pltpu.VMEM((held, slots, width), BF16),
            pltpu.VMEM(w_gate.shape, BF16),
            pltpu.VMEM(w_up.shape, BF16),
        ]
        + scratch(spans[0])
        + [pltpu.SemaphoreType.DMA((2, held)), pltpu.SemaphoreType.DMA((tensors, held))],
        compiler_params=pltpu.CompilerParams(vmem_limit_bytes=56 * 1024 * 1024),
        name="experts_first",
    )(placing, back, *pieces, w_gate, w_up, w_down)

    more = sum(spans[1:])
    outs += pl.pallas_call(
        functools.partial(later_kernel, (cores, tensors, groups, spans[0], spans[1:])),
        out_shape=[shape for span in spans[1:] for shape in out_shapes(span)],
        in_specs=[VMEM, VMEM, HBM],
        out_specs=[VMEM] * (cores * tensors * len(spans[1:])),
        scratch_shapes=scratch(more) + [pltpu.SemaphoreType.DMA((tensors, held))],
        compiler_params=PARAMS,
        cost_estimate=pl.CostEstimate(
            flops=4 * slots * held * hidden_units * more * tensors,
            bytes_accessed=2 * held * hidden_units * more * tensors,
            transcendentals=0,
        ),
        name="experts_later",
    )(back, activated, w_down)
    results = []
    for n, span in enumerate(spans):
        mixed = outs[n * cores * tensors :]
        sides = []
        for t in list(range(1, tensors)) + [0]:
            summed = mixed[t].astype(F32)
            for i in range(1, cores):
                got = fetch(mixed[i * tensors + t], "dp", -i)
                summed = summed + got.astype(F32)
            if t > 0:
                got = fetch(summed.astype(BF16), "tensor", -t)
                sides.append(got)
        narrow = summed
        for got in sides:
            narrow = narrow + got.astype(F32)
        narrow = narrow.reshape(depth, rows, span)
        flip = 1
        if depth == 4 and n + 1 == len(spans):
            whole = narrow[0]
            for o in range(1, depth):
                got = across(narrow[o].astype(BF16), "expert", o)
                whole = whole + got.astype(F32)
            results.append(whole.astype(BF16))
            continue
        while flip < depth:
            narrow = narrow.reshape(-1, 2, rows, span)
            got = across(narrow[:, 1].astype(BF16), "expert", flip)
            narrow = narrow[:, 0] + got.astype(F32)
            flip *= 2
        results.append(narrow[0].astype(BF16))
    return jnp.concatenate(results, axis=1)


def solution(mesh):
    placed = (
        P(("groups", "expert", "dp"), "tensor"),
        P("tensor", "dp"),
        P(("groups", "expert", "dp"), "tensor"),
        P(),
        P(("groups", "expert", "dp"), None),
        P(("groups", "expert", "dp"), None),
        P(("expert", "dp"), None, "tensor"),
        P(("expert", "dp"), None, "tensor"),
        P(("expert", "dp"), "tensor", None),
    )

    step = jax.shard_map(
        on_device,
        mesh=mesh,
        in_specs=placed,
        out_specs=P(("groups", "expert", "dp"), "tensor"),
        check_vma=False,
    )
    if mesh.shape["tensor"] != mesh.shape["dp"]:
        return step
    return step
```
